32 devices in a mesh: sub: 16 (over z, y, core), shot: 2 (over x).
Axes of the slice: x: 2, y: 2, z: 4, core: 2. Of those that a mesh axis runs over, the one named last changes fastest.
Arguments:
- courant: float32 [256, 64, 128], P('sub'), may hold values from 0.02 to 0.18
- wave_now: float32 [2, 2, 256, 64, 128], P(None, 'shot', 'sub'), may hold values from -4 to 4
- wave_later: float32 [2, 2, 256, 64, 128], P(None, 'shot', 'sub'), may hold values from -4 to 4
- traces: float32 [2, 3, 8192], P('shot', None, 'sub'), may hold values from -6 to 6
- rec_owner: int32 [2, 8192, 1], P('shot', 'sub'), may hold values from 0 to 15; in each aligned block of 512 rows (0 to 511, 512 to 1023, ..., all dimensions but the last counted through in order) at most 64 rows name the same one
- rec_cell: int32 [2, 8192], P('shot', 'sub'), may hold values from 0 to 131071
- source_x: int32 [2], P('shot'), may hold values from 0 to 255
- source_yz: int32 [2], P('shot'), may hold values from 0 to 8191
- wavelet: float32 [2, 3], P('shot'), may hold values from -8 to 8
- aperture: int32 [2, 16], P('shot'), may hold values 0 or 1
Outputs:
- image: float32 [256, 64, 128], P('sub', 'shot')
- wave_final: float32 [2, 2, 256, 64, 128], P(None, 'shot', 'sub')
The draws below stay inside these ranges and needn't reach their ends.
Inputs may be any that keep to these rules, and one draw needn't show every extreme that they name: `rec_owner`: among the receivers of one shot held by one index of sub, at most 64 have the same owner, and in some such block exactly 64 do.
All inputs are finite; a program needn't handle non-finite values. No bound on the sum of `aperture` on one device may be relied on, other than what follows from the above.
Results may differ from the reference program's by a relative error of at most 0.0003.
Values sent between devices are 32-bit elements; how exact they have to be, the bound alone decides.
A program may use at most 64 MiB of HBM per device.

```python
import math
import jax
import jax.numpy as jnp
import numpy as np
from jax import lax

CX = 16
NY = 64
NZ = 128
REC_DEV = 512
STEPS = 3
NX = 256
SHOTS = 2
RECS = 8192
CAP = 64
N_SUB = 16


def with_ends(drawn, own_key, least, high):
    extent = drawn.shape
    index_at = [jax.random.randint(jax.random.fold_in(own_key, axis), (), 0, extent[axis]) for axis in range(len(extent))]
    drawn = drawn.at[tuple(index_at)].set(least)
    longest = extent.index(max(extent))
    index_at[longest] = (index_at[longest] + 1) % extent[longest]
    return drawn.at[tuple(index_at)].set(high)


def block_scale(rng, dims, shards, least, high):
    level, own = 1.0, jax.random.fold_in(rng, 6)
    for axis_at, parts in shards:
        draws = jnp.exp(jax.random.uniform(jax.random.fold_in(own, axis_at), (parts,), jnp.float32, least / len(shards), high / len(shards)))
        level = level * jnp.repeat(draws, dims[axis_at] // parts).reshape([-1 if axis == axis_at else 1 for axis in range(len(dims))])
    return level


def shared_out(stream_key, own, number, rows, number_of, top, most, lean):
    sequence = jax.random.permutation(stream_key, number_of)
    packed, common = portions_of(number_of, rows * top, most, lean, True), portions_of(number_of, rows * top, most, lean, False)
    places = jnp.arange(number_of)

    def named(lengths, offset_by):
        used = int((lengths > 0).sum())
        fixed = max(1, used // 4)
        passed = fixed + (places - fixed + offset_by * (used - fixed)) % max(1, number_of - fixed)
        return jnp.zeros((number_of,), jnp.int32).at[sequence[jnp.where(places < fixed, places, passed)]].set(jnp.asarray(lengths, jnp.int32))

    lengths = jnp.where(number % 4 == 0, named(packed, number // 4), named(common, number - number // 4 - 1))
    mixed = jax.random.permutation(jax.random.fold_in(own, 3), number_of)
    donor, taker = mixed[0:number_of // 2 * 2:2], mixed[1:number_of // 2 * 2:2]
    margin = jnp.minimum(lengths[donor] - 1, most - lengths[taker]) // 2
    margin = jnp.where((donor == sequence[0]) | (taker == sequence[0]) | (lengths[taker] == 0), 0, jnp.maximum(margin, 0))
    passed = jax.random.randint(jax.random.fold_in(own, 4), (number_of // 2,), 0, 1 << 20) % (margin + 1)
    lengths = lengths.at[donor].add(-passed).at[taker].add(passed)
    items = jnp.searchsorted(jnp.cumsum(lengths), jnp.arange(rows * top), side="right").astype(jnp.int32)
    grid = items.reshape(top, rows).T
    grid = grid[jax.random.permutation(jax.random.fold_in(own, 1), rows)]
    offset_by = jax.random.randint(jax.random.fold_in(own, 2), (rows, 1), 0, top)
    return jnp.take_along_axis(grid, (jnp.arange(top)[None, :] + offset_by) % top, axis=1)


def portions_of(number_of, total, reach, slope, full):
    portions = [(1 << 20) // math.isqrt(standing ** slope) + 1 for standing in range(1, number_of + 1)]
    largest = reach if full else min(reach, max(-(-total // number_of), total * portions[0] // sum(portions)))
    least = 1 if total - largest >= number_of - 1 else 0
    holding, rest = [largest] + [least] * (number_of - 1), total - largest - least * (number_of - 1)
    while rest > 0:
        free = [i for i in range(1, number_of) if holding[i] < largest] or [i for i in range(1, number_of) if holding[i] < reach]
        mass, remaining = sum([portions[i] for i in free]), rest
        for i in free:
            extra = min(reach - holding[i], max(1, remaining * portions[i] // mass), rest)
            holding[i] = holding[i] + extra
            rest = rest - extra
    return np.array(holding)


def centred(key, shape, scale, bound, split=(), held_as=jnp.bfloat16):
    values = scale * jax.random.normal(key, shape, jnp.float32)
    if split:
        values = values * block_scale(key, shape, split, -0.22, 0.18)
    return jnp.clip(values, -bound, bound).astype(held_as)


def setup_inputs(seed: int = 0) -> dict:
    streams_of = jax.random.split(jax.random.key(seed), 11)
    courant = jnp.clip(jnp.exp(math.log(0.18) - 2.1972246 * jax.random.uniform(streams_of[0], (NX, NY, NZ), jnp.float32) ** block_scale(streams_of[0], (NX, NY, NZ), ((0, 16),), -0.2, 0.2)), 0.02, 0.18)
    wave_now = centred(streams_of[1], (2, SHOTS, NX, NY, NZ), 0.5, 4.0, ((1, 2), (2, 16)), jnp.float32)
    wave_later = centred(streams_of[2], (2, SHOTS, NX, NY, NZ), 0.5, 4.0, ((1, 2), (2, 16)), jnp.float32)
    traces = centred(streams_of[3], (SHOTS, STEPS, RECS), 1.0, 6.0, ((0, 2), (2, 16)), jnp.float32)
    rec_owner_keys = jax.random.split(jax.random.fold_in(streams_of[4], 1), SHOTS * RECS // REC_DEV)
    rec_owner_turns = jax.random.permutation(jax.random.fold_in(streams_of[4], 3), SHOTS * RECS // REC_DEV)
    rec_owner = jax.vmap(lambda own, number: shared_out(jax.random.fold_in(streams_of[4], 2), own, number, REC_DEV, N_SUB, 1, CAP, 2))(rec_owner_keys, rec_owner_turns).reshape((SHOTS, RECS, 1))
    rec_cell = with_ends(jax.random.randint(streams_of[5], (SHOTS, RECS), 0, CX * NY * NZ), jax.random.fold_in(streams_of[5], 1), 0, (CX * NY * NZ) - 1).astype(jnp.int32)
    source_x = jax.random.randint(streams_of[6], (SHOTS,), 0, NX).astype(jnp.int32)
    source_yz = jax.random.randint(streams_of[7], (SHOTS,), 0, NY * NZ).astype(jnp.int32)
    wavelet = centred(streams_of[8], (SHOTS, STEPS), 2.0, 8.0, ((0, 2),), jnp.float32)
    aperture = with_ends((jax.random.randint(streams_of[9], (SHOTS, N_SUB), 0, 4) < 3).astype(jnp.int32), jax.random.fold_in(streams_of[9], 1), 0, 1)
    return {"courant": courant, "wave_now": wave_now, "wave_later": wave_later, "traces": traces, "rec_owner": rec_owner, "rec_cell": rec_cell, "source_x": source_x, "source_yz": source_yz, "wavelet": wavelet, "aperture": aperture}


STENCIL = (-205.0 / 72.0, 8.0 / 5.0, -1.0 / 5.0, 8.0 / 315.0, -1.0 / 560.0)


def laplace(wavefield):
    extent_x, extent_y, extent_z = wavefield.shape
    padded = jnp.pad(wavefield, 4)
    summed = 3.0 * STENCIL[0] * wavefield
    for offset in range(1, 5):
        weight = STENCIL[offset]
        summed = summed + weight * (padded[4 + offset:4 + offset + extent_x, 4:4 + extent_y, 4:4 + extent_z]
                                    + padded[4 - offset:4 - offset + extent_x, 4:4 + extent_y, 4:4 + extent_z])
        summed = summed + weight * (padded[4:4 + extent_x, 4 + offset:4 + offset + extent_y, 4:4 + extent_z]
                                    + padded[4:4 + extent_x, 4 - offset:4 - offset + extent_y, 4:4 + extent_z])
        summed = summed + weight * (padded[4:4 + extent_x, 4:4 + extent_y, 4 + offset:4 + offset + extent_z]
                                    + padded[4:4 + extent_x, 4:4 + extent_y, 4 - offset:4 - offset + extent_z])
    return summed


def reference(courant, wave_now, wave_later, traces, rec_owner, rec_cell, source_x, source_yz, wavelet, aperture):
    cell_count = CX * NY * NZ
    global_x = jnp.arange(NX, dtype=jnp.int32)
    tile_of = global_x // CX
    yz_cells = jnp.arange(NY * NZ, dtype=jnp.int32)

    def one_shot(shot_index):
        source_now = wave_now[0, shot_index]
        source_later = wave_later[0, shot_index]
        receiver_now = wave_now[1, shot_index]
        receiver_later = wave_later[1, shot_index]
        flat_cells = (rec_owner[shot_index, :, 0] * cell_count + rec_cell[shot_index]).astype(jnp.int32)
        aperture_x = aperture[shot_index].astype(jnp.float32)[tile_of]
        source_grid = ((global_x == source_x[shot_index]).astype(jnp.float32)[:, None]
                       * (yz_cells == source_yz[shot_index]).astype(jnp.float32)[None, :]).reshape(NX, NY, NZ)
        image_part = jnp.zeros((NX, NY, NZ), jnp.float32)
        for step_index in range(STEPS):
            source_next = (2.0 * source_now - source_later + courant * laplace(source_now)
                           - wavelet[shot_index, step_index] * source_grid)
            injected = jnp.zeros((NX * NY * NZ,), jnp.float32).at[flat_cells].add(
                traces[shot_index, step_index]).reshape(NX, NY, NZ)
            receiver_next = 2.0 * receiver_now - receiver_later + courant * laplace(receiver_now) + injected
            image_part = image_part + aperture_x[:, None, None] * source_next * receiver_next
            source_later, source_now = source_now, source_next
            receiver_later, receiver_now = receiver_now, receiver_next
        return jnp.stack([source_now, receiver_now]), image_part

    finals, images = lax.map(one_shot, jnp.arange(SHOTS, dtype=jnp.int32))
    return jnp.sum(images, axis=0), jnp.moveaxis(finals, 0, 1)
```

```python
import functools

import jax
import jax.numpy as jnp
from jax import lax
from jax.experimental import pallas as pl
from jax.experimental.pallas import tpu as pltpu
from jax.sharding import PartitionSpec as P

STENCIL = (-205.0 / 72.0, 8.0 / 5.0, -1.0 / 5.0, 8.0 / 315.0, -1.0 / 560.0)
REACH = len(STENCIL) - 1
MARGIN = 8
LANES = 128
SUBLANES = 8
MESH = pl.DeviceIdType.MESH
NT = (((1,), (1,)), ((), ()))


def iota(shape, dim):
    return lax.broadcasted_iota(jnp.int32, shape, dim)


def onehot(mask):
    return jnp.where(mask, 1.0, 0.0).astype(jnp.bfloat16)


def rounded(x):
    return x.astype(jnp.bfloat16).astype(jnp.float32)


def kernel(
    sub_count,
    shot_count,
    step_count,
    wavelet_hbm,
    source_x_hbm,
    source_yz_hbm,
    aperture_hbm,
    owner_hbm,
    cell_hbm,
    trace_hbm,
    courant_hbm,
    now_hbm,
    later_hbm,
    image_out,
    final,
    wavelet_ref,
    source_x_ref,
    source_yz_ref,
    aperture_ref,
    owner_ref,
    cell_ref,
    trace_ref,
    small_sem,
    state,
    halo,
    band,
    along,
    later,
    courant,
    inj,
    image,
    image_in,
    terms,
    packed_terms,
    packed,
    arrived,
    slots,
    spread,
    load_sem,
    halo_send,
    halo_recv,
    swap_send,
    swap_recv,
    image_send,
    image_recv,
):
    span, cells_y, cells_z = courant.shape
    receivers = owner_ref.shape[1]
    capacity = max(2, 2 * receivers // sub_count)
    group = max(1, min(LANES // capacity, sub_count))
    own_rows = cells_y // shot_count
    me = lax.axis_index("sub")
    shot = lax.axis_index("shot")
    has_before = me > 0
    has_after = me < sub_count - 1
    inside_y = pl.ds(MARGIN, cells_y)

    barrier = pltpu.get_barrier_semaphore()
    for offset in range(1, sub_count):
        pl.semaphore_signal(
            barrier,
            inc=1,
            device_id={"sub": lax.rem(me + offset, sub_count)},
            device_id_type=MESH,
        )
    for offset in range(1, shot_count):
        pl.semaphore_signal(
            barrier,
            inc=1,
            device_id={"shot": lax.rem(shot + offset, shot_count)},
            device_id_type=MESH,
        )

    small_loads = [
        pltpu.make_async_copy(source, target, small_sem.at[index])
        for index, (source, target) in enumerate(
            (
                (owner_hbm, owner_ref),
                (cell_hbm, cell_ref),
                (trace_hbm, trace_ref),
                (wavelet_hbm, wavelet_ref),
                (source_x_hbm, source_x_ref),
                (source_yz_hbm, source_yz_ref),
                (aperture_hbm, aperture_ref),
            )
        )
    ]
    for load in small_loads:
        load.start()
    loads = [
        pltpu.make_async_copy(
            now_hbm.at[field, 0],
            state.at[0, field, :, inside_y, :],
            load_sem.at[field],
        )
        for field in range(2)
    ]
    loads.append(pltpu.make_async_copy(later_hbm.at[:, 0], later, load_sem.at[2]))
    loads.append(pltpu.make_async_copy(courant_hbm, courant, load_sem.at[3]))
    for load in loads:
        load.start()

    def halo_copy(step, field, side):
        first = side * (span - REACH)
        if step == 0:
            source = now_hbm.at[field, 0, pl.ds(first, REACH)]
        else:
            source = state.at[step, field, pl.ds(first, REACH), inside_y, :]
        return pltpu.make_async_remote_copy(
            src_ref=source,
            dst_ref=halo.at[step, field, 1 - side],
            send_sem=halo_send.at[step, field, side],
            recv_sem=halo_recv.at[step, field, 1 - side],
            device_id={"sub": lax.rem(me + sub_count - 1 + 2 * side, sub_count)},
            device_id_type=MESH,
        )

    reaches = (has_before, has_after)

    def halo_start(step, field, side):
        @pl.when(reaches[side])
        def _():
            halo_copy(step, field, side).start()

    def halo_wait(step, field, side):
        @pl.when(reaches[side])
        def _():
            halo_copy(step, field, 1 - side).wait_recv()

    def halo_sent(step, field, side):
        @pl.when(reaches[side])
        def _():
            halo_copy(step, field, side).wait_send()

    pl.semaphore_wait(barrier, sub_count - 1 + shot_count - 1)


    for side in range(2):
        halo_start(0, 0, side)

    def clear_margins(index, carry):
        zero = jnp.zeros((MARGIN, cells_z), jnp.float32)
        for step in range(step_count):
            for field in range(2):
                state[step, field, index, pl.ds(0, MARGIN), :] = zero
                state[step, field, index, pl.ds(MARGIN + cells_y, MARGIN), :] = zero
        return carry

    lax.fori_loop(0, span, clear_margins, 0)

    def clear_halo(side):
        for step in range(step_count):
            for field in range(2):
                for plane in range(REACH):
                    halo[step, field, side, plane] = jnp.zeros((cells_y, cells_z), jnp.float32)

    @pl.when(jnp.logical_not(has_before))
    def _():
        clear_halo(0)

    @pl.when(jnp.logical_not(has_after))
    def _():
        clear_halo(1)

    apart = jnp.abs(iota((cells_z, cells_z), 0) - iota((cells_z, cells_z), 1))
    weights = jnp.where(apart == 0, 3.0 * STENCIL[0], 0.0)
    for offset in range(1, REACH + 1):
        weights = jnp.where(apart == offset, STENCIL[offset], weights)
    for column, weight in enumerate((rounded(weights), weights - rounded(weights))):
        for first in (0, cells_z):
            band[pl.ds(first, cells_z), pl.ds(column * cells_z, cells_z)] = weight.astype(
                jnp.bfloat16
            )

    for load in small_loads:
        load.wait()
    owner = owner_ref[...]
    cell = cell_ref[...]
    named = jnp.where(iota((sub_count, receivers), 0) == owner, 1.0, 0.0)
    earlier = onehot(iota((receivers, receivers), 0) < iota((receivers, receivers), 1))
    counts = jnp.dot(named.astype(jnp.bfloat16), earlier, preferred_element_type=jnp.float32)
    ranking = jnp.sum(counts * named, axis=0, keepdims=True).astype(jnp.int32)
    slot = owner * LANES + lax.rem(me, group) * capacity + ranking
    part = trace_ref[:, 0, :]
    width = step_count + 1
    terms[...] = jnp.zeros_like(terms)
    for third in range(3):
        high = rounded(part)
        terms[pl.ds(third * width, step_count), :] = high
        part = part - high
    terms[pl.ds(step_count, 1), :] = (lax.shift_right_logical(cell, 16) * 65536).astype(jnp.float32)
    terms[pl.ds(width + step_count, 1), :] = (
        jnp.bitwise_and(lax.shift_right_logical(cell, 8), 255) * 256
    ).astype(jnp.float32)
    terms[pl.ds(2 * width + step_count, 1), :] = jnp.bitwise_and(cell, 255).astype(jnp.float32)
    stacked = terms[...].astype(jnp.bfloat16)
    chunk = 4 * LANES
    for first in range(0, sub_count * LANES, chunk):
        picks = onehot(iota((chunk, receivers), 0) + first == slot)
        packed_terms[:, pl.ds(first, chunk)] = lax.dot_general(
            stacked, picks, NT, preferred_element_type=jnp.float32
        )
    for peer in range(sub_count):
        lanes = pl.ds(peer * LANES, LANES)
        packed[peer] = (
            packed_terms[pl.ds(0, width), lanes]
            + packed_terms[pl.ds(width, width), lanes]
            + packed_terms[pl.ds(2 * width, width), lanes]
        )

    swaps = []
    for offset in range(1, sub_count):
        peer = lax.rem(me + offset, sub_count)
        swaps.append(
            pltpu.make_async_remote_copy(
                src_ref=packed.at[peer],
                dst_ref=arrived.at[offset],
                send_sem=swap_send.at[offset],
                recv_sem=swap_recv.at[offset],
                device_id={"sub": peer},
                device_id_type=MESH,
            )
        )
    for swap in swaps:
        swap.start()
    for side in range(2):
        halo_start(0, 1, side)
    arrived[0] = packed[me]

    place = iota((SUBLANES, cells_z), 0) * cells_z + iota((SUBLANES, cells_z), 1)
    source_plane = source_x_ref[0, 0] - me * span
    source_place = source_yz_ref[0, 0]

    def put(step, field, plane, rows, value):
        if step == step_count - 1:
            final[field, 0, plane, rows, :] = value
        else:
            state[step + 1, field, plane, pl.ds(rows.start + MARGIN, rows.size), :] = value

    planes_at_once = 16

    def advance(step, field):
        def depth_part(index, carry):
            first = pl.multiple_of(index * planes_at_once, planes_at_once)
            value = state[step, field, pl.ds(first, planes_at_once), inside_y, :]
            value = value.reshape(planes_at_once * cells_y, cells_z)
            high = value.astype(jnp.bfloat16)
            low = (value - high.astype(jnp.float32)).astype(jnp.bfloat16)
            both = jnp.dot(
                jnp.concatenate([high, low], axis=1),
                band[...],
                preferred_element_type=jnp.float32,
            )
            total = both[:, :cells_z] + both[:, cells_z:]
            along[pl.ds(first, planes_at_once)] = total.reshape(planes_at_once, cells_y, cells_z)
            return carry

        lax.fori_loop(0, span // planes_at_once, depth_part, 0)

        def one_row(index, carry):
            first = pl.multiple_of(index * SUBLANES, SUBLANES)
            rows = pl.ds(first, SUBLANES)
            shifted = pl.ds(first + MARGIN, SUBLANES)
            column = [state[step, field, plane, shifted, :] for plane in range(span)]
            if field == 0:
                source_here = jnp.where(
                    place + first * cells_z == source_place, wavelet_ref[0, step], 0.0
                )
            for plane in range(span):
                total = along[plane, rows, :]
                for offset in range(1, REACH + 1):
                    near = (
                        state[step, field, plane, pl.ds(first + MARGIN + offset, SUBLANES), :]
                        + state[step, field, plane, pl.ds(first + MARGIN - offset, SUBLANES), :]
                    )
                    for other in (plane - offset, plane + offset):
                        if 0 <= other < span:
                            near = near + column[other]
                    total = total + STENCIL[offset] * near
                if step == 0:
                    past = later[field, plane, rows, :]
                else:
                    past = state[step - 1, field, plane, shifted, :]
                stepped = 2.0 * column[plane] - past + courant[plane, rows, :] * total
                if field == 0:
                    stepped = stepped - jnp.where(plane == source_plane, 1.0, 0.0) * source_here
                else:
                    stepped = stepped + inj[step, pl.ds(plane * cells_y + first, SUBLANES), :]
                put(step, field, plane, rows, stepped)
            return carry

        lax.fori_loop(0, cells_y // SUBLANES, one_row, 0)

    def add_halo(step, field, side):
        base = side * (span - REACH)

        def one_row(index, carry):
            first = pl.multiple_of(index * SUBLANES, SUBLANES)
            rows = pl.ds(first, SUBLANES)
            shifted = pl.ds(first + MARGIN, SUBLANES)
            outside = [halo[step, field, side, plane, rows, :] for plane in range(REACH)]
            for plane in range(REACH):
                total = jnp.zeros((SUBLANES, cells_z), jnp.float32)
                for other in range(REACH):
                    distance = other + REACH - plane if side else plane + REACH - other
                    if distance <= REACH:
                        total = total + STENCIL[distance] * outside[other]
                if step == step_count - 1:
                    value = final[field, 0, base + plane, rows, :]
                else:
                    value = state[step + 1, field, base + plane, shifted, :]
                value = value + courant[base + plane, rows, :] * total
                put(step, field, base + plane, rows, value)
            return carry

        lax.fori_loop(0, cells_y // SUBLANES, one_row, 0)

    def by_distance(act):
        even = lax.rem(me, 2) == 0

        @pl.when(even)
        def _():
            act(1)

        @pl.when(jnp.logical_not(even))
        def _():
            act(0)

        @pl.when(even)
        def _():
            act(0)

        @pl.when(jnp.logical_not(even))
        def _():
            act(1)

    loads[0].wait()
    loads[2].wait()
    loads[3].wait()
    advance(0, 0)

    def receive():
        for swap in swaps:
            swap.wait_recv()
        for first in range(0, sub_count, group):
            joined = arrived[first]
            for other in range(1, group):
                joined = joined + arrived[first + other]
            slots[:, pl.ds(first // group * LANES, LANES)] = joined
        slot_count = slots.shape[1]
        here = slots[pl.ds(step_count, 1), :].astype(jnp.int32)
        row = here // cells_z
        depth = here - row * cells_z
        at_depth = iota((cells_z, slot_count), 0) == depth
        for step in range(step_count):
            value = slots[pl.ds(step, 1), :]
            high = rounded(value)
            low = value - high
            first = 2 * step * cells_z
            spread[pl.ds(first, cells_z), :] = jnp.where(at_depth, high, 0.0).astype(jnp.bfloat16)
            spread[pl.ds(first + cells_z, cells_z), :] = jnp.where(at_depth, low, 0.0).astype(
                jnp.bfloat16
            )
        row_chunk = 256

        def deposit(index, carry):
            first = pl.multiple_of(index * row_chunk, row_chunk)
            at_row = onehot(iota((row_chunk, slot_count), 0) + first == row)
            for step in range(step_count):
                both = lax.dot_general(
                    at_row,
                    spread[pl.ds(2 * step * cells_z, 2 * cells_z), :],
                    NT,
                    preferred_element_type=jnp.float32,
                )
                inj[step, pl.ds(first, row_chunk), :] = both[:, :cells_z] + both[:, cells_z:]
            return carry

        lax.fori_loop(0, span * cells_y // row_chunk, deposit, 0)

    aperture_here = aperture_ref[0, me].astype(jnp.float32)

    def image_planes(first, count):
        def one_plane(index, carry):
            plane = index + first
            total = final[0, 0, plane] * final[1, 0, plane]
            for step in range(1, step_count):
                total = total + (
                    state[step, 0, plane, inside_y, :] * state[step, 1, plane, inside_y, :]
                )
            image[plane] = aperture_here * total
            return carry

        lax.fori_loop(0, count, one_plane, 0)

    portions = (
        (REACH, span - 2 * REACH),
        (0, REACH),
        (span - REACH, REACH),
    )

    def image_copies(portion):
        first, count = portions[portion]
        copies = []
        for offset in range(1, shot_count):
            peer = lax.rem(shot + offset, shot_count)
            rows = pl.ds(pl.multiple_of(peer * own_rows, own_rows), own_rows)
            copies.append(
                pltpu.make_async_remote_copy(
                    src_ref=image.at[pl.ds(first, count), rows, :],
                    dst_ref=image_in.at[offset - 1, pl.ds(first, count)],
                    send_sem=image_send.at[portion, offset - 1],
                    recv_sem=image_recv.at[portion, offset - 1],
                    device_id={"shot": peer},
                    device_id_type=MESH,
                )
            )
        return copies

    def image_join(portion):
        first, count = portions[portion]
        for copy in image_copies(portion):
            copy.wait_recv()
        rows = pl.ds(pl.multiple_of(shot * own_rows, own_rows), own_rows)

        def one_plane(index, carry):
            plane = index + first
            total = image[plane, rows, :]
            for offset in range(1, shot_count):
                total = total + image_in[offset - 1, plane]
            image_out[plane] = total
            return carry

        lax.fori_loop(0, count, one_plane, 0)

    def image_start(portion):
        image_planes(*portions[portion])
        for copy in image_copies(portion):
            copy.start()

    for step in range(step_count):
        last = step == step_count - 1
        for field in range(2):

            def arrive(side, step=step, field=field, last=last):
                halo_wait(step, field, side)
                add_halo(step, field, side)
                if not last:
                    halo_start(step + 1, field, side)
                elif field == 1:
                    image_start(1 + side)

            by_distance(arrive)
            if step == 0 and field == 0:
                receive()
                loads[1].wait()
                advance(0, 1)
            if not last:
                advance(step + 1, field)
        if step == step_count - 2:
            image_start(0)
    for portion in range(3):
        image_join(portion)
    for swap in swaps:
        swap.wait_send()
    for step in range(step_count):
        for field in range(2):
            for side in range(2):
                halo_sent(step, field, side)
    for portion in range(3):
        for copy in image_copies(portion):
            copy.wait_send()


def local(
    courant,
    wave_now,
    wave_later,
    traces,
    rec_owner,
    rec_cell,
    source_x,
    source_yz,
    wavelet,
    aperture,
):
    span, cells_y, cells_z = courant.shape
    sub_count = lax.axis_size("sub")
    shot_count = lax.axis_size("shot")
    step_count, receivers = traces.shape[1:]
    capacity = max(2, 2 * receivers // sub_count)
    group = max(1, min(LANES // capacity, sub_count))
    slot_count = sub_count // group * LANES
    terms_height = -(-3 * (step_count + 1) // 16) * 16
    vmem = pl.BlockSpec(memory_space=pltpu.VMEM)
    hbm = pl.BlockSpec(memory_space=pl.ANY)
    dma = pltpu.SemaphoreType.DMA
    image, final = pl.pallas_call(
        functools.partial(kernel, sub_count, shot_count, step_count),
        out_shape=(
            pltpu.VMEM((span, cells_y // shot_count, cells_z), jnp.float32),
            pltpu.VMEM(wave_now.shape, jnp.float32),
        ),
        in_specs=[hbm] * 10,
        out_specs=(vmem, vmem),
        scratch_shapes=[
            pltpu.SMEM(wavelet.shape, jnp.float32),
            pltpu.SMEM((1, 1), jnp.int32),
            pltpu.SMEM((1, 1), jnp.int32),
            pltpu.SMEM(aperture.shape, jnp.int32),
            pltpu.VMEM((1, receivers), jnp.int32),
            pltpu.VMEM((1, receivers), jnp.int32),
            pltpu.VMEM((step_count, 1, receivers), jnp.float32),
            dma((7,)),
            pltpu.VMEM(
                (step_count, 2, span, cells_y + 2 * MARGIN, cells_z), jnp.float32
            ),
            pltpu.VMEM((step_count, 2, 2, REACH, cells_y, cells_z), jnp.float32),
            pltpu.VMEM((2 * cells_z, 2 * cells_z), jnp.bfloat16),
            pltpu.VMEM((span, cells_y, cells_z), jnp.float32),
            pltpu.VMEM((2, span, cells_y, cells_z), jnp.float32),
            pltpu.VMEM((span, cells_y, cells_z), jnp.float32),
            pltpu.VMEM((step_count, span * cells_y, cells_z), jnp.float32),
            pltpu.VMEM((span, cells_y, cells_z), jnp.float32),
            pltpu.VMEM(
                (max(1, shot_count - 1), span, cells_y // shot_count, cells_z), jnp.float32
            ),
            pltpu.VMEM((terms_height, receivers), jnp.float32),
            pltpu.VMEM((terms_height, sub_count * LANES), jnp.float32),
            pltpu.VMEM((sub_count, step_count + 1, LANES), jnp.float32),
            pltpu.VMEM((sub_count, step_count + 1, LANES), jnp.float32),
            pltpu.VMEM((step_count + 1, slot_count), jnp.float32),
            pltpu.VMEM((2 * step_count * cells_z, slot_count), jnp.bfloat16),
            dma((4,)),
            dma((step_count, 2, 2)),
            dma((step_count, 2, 2)),
            dma((sub_count,)),
            dma((sub_count,)),
            dma((3, max(1, shot_count - 1))),
            dma((3, max(1, shot_count - 1))),
        ],
        compiler_params=pltpu.CompilerParams(collective_id=0, has_side_effects=True),
    )(
        wavelet,
        source_x.reshape(1, 1),
        source_yz.reshape(1, 1),
        aperture,
        rec_owner.reshape(1, receivers),
        rec_cell,
        jnp.transpose(traces, (1, 0, 2)),
        courant,
        wave_now,
        wave_later,
    )
    return image, final


def solution(mesh):
    in_specs = (
        P("sub", None, None),
        P(None, "shot", "sub", None, None),
        P(None, "shot", "sub", None, None),
        P("shot", None, "sub"),
        P("shot", "sub", None),
        P("shot", "sub"),
        P("shot"),
        P("shot"),
        P("shot", None),
        P("shot", None),
    )
    out_specs = (P("sub", "shot", None), P(None, "shot", "sub", None, None))
    return jax.shard_map(local, mesh=mesh, in_specs=in_specs, out_specs=out_specs, check_vma=False)
```

```python
import functools

import jax
import jax.numpy as jnp
from jax import lax
from jax.experimental import pallas as pl
from jax.experimental.pallas import tpu as pltpu
from jax.sharding import PartitionSpec as P

STENCIL = (-205.0 / 72.0, 8.0 / 5.0, -1.0 / 5.0, 8.0 / 315.0, -1.0 / 560.0)
REACH = len(STENCIL) - 1
MARGIN = 8
LANES = 128
SUBLANES = 8
MESH = pl.DeviceIdType.MESH
NT = (((1,), (1,)), ((), ()))


def iota(shape, dim):
    return lax.broadcasted_iota(jnp.int32, shape, dim)


def onehot(mask):
    return jnp.where(mask, 1.0, 0.0).astype(jnp.bfloat16)


def rounded(x):
    return x.astype(jnp.bfloat16).astype(jnp.float32)


def kernel(
    sub_count,
    shot_count,
    step_count,
    wavelet_hbm,
    source_x_hbm,
    source_yz_hbm,
    aperture_hbm,
    owner_hbm,
    cell_hbm,
    trace_hbm,
    courant_hbm,
    now_hbm,
    later_hbm,
    image_out,
    final,
    wavelet_ref,
    source_x_ref,
    source_yz_ref,
    aperture_ref,
    owner_ref,
    cell_ref,
    trace_ref,
    small_sem,
    state,
    halo,
    band,
    along,
    later,
    courant,
    inj,
    image,
    image_in,
    terms,
    packed_terms,
    packed,
    arrived,
    slots,
    spread,
    at_row,
    load_sem,
    halo_send,
    halo_recv,
    half_send,
    half_recv,
    swap_send,
    swap_recv,
    image_send,
    image_recv,
):
    span, cells_y, cells_z = courant.shape
    receivers = owner_ref.shape[1]
    capacity = max(2, 2 * receivers // sub_count)
    group = max(1, min(LANES // capacity, sub_count))
    own_rows = cells_y // shot_count
    me = lax.axis_index("sub")
    shot = lax.axis_index("shot")
    half_rows = cells_y // 2
    half_shots = shot_count // 2
    own_half = shot // half_shots
    halves = tuple(
        pl.multiple_of(half * half_rows, half_rows) for half in (1 - own_half, own_half)
    )
    has_before = me > 0
    has_after = me < sub_count - 1
    inside_y = pl.ds(MARGIN, cells_y)

    barrier = pltpu.get_barrier_semaphore()
    for offset in range(1, sub_count):
        pl.semaphore_signal(
            barrier,
            inc=1,
            device_id={"sub": lax.rem(me + offset, sub_count)},
            device_id_type=MESH,
        )
    for offset in range(1, shot_count):
        pl.semaphore_signal(
            barrier,
            inc=1,
            device_id={"shot": lax.rem(shot + offset, shot_count)},
            device_id_type=MESH,
        )

    small_loads = [
        pltpu.make_async_copy(source, target, small_sem.at[index])
        for index, (source, target) in enumerate(
            (
                (owner_hbm, owner_ref),
                (cell_hbm, cell_ref),
                (trace_hbm, trace_ref),
                (wavelet_hbm, wavelet_ref),
                (source_x_hbm, source_x_ref),
                (source_yz_hbm, source_yz_ref),
                (aperture_hbm, aperture_ref),
            )
        )
    ]
    for load in small_loads:
        load.start()
    loads = [
        pltpu.make_async_copy(
            now_hbm.at[field, 0],
            state.at[0, field, :, inside_y, :],
            load_sem.at[field],
        )
        for field in range(2)
    ]
    loads.append(pltpu.make_async_copy(later_hbm.at[:, 0], later, load_sem.at[2]))
    loads.append(pltpu.make_async_copy(courant_hbm, courant, load_sem.at[3]))
    for load in loads:
        load.start()

    def halo_copy(step, field, side):
        first = side * (span - REACH)
        if step == 0:
            source = now_hbm.at[field, 0, pl.ds(first, REACH)]
        else:
            source = state.at[step, field, pl.ds(first, REACH), inside_y, :]
        return pltpu.make_async_remote_copy(
            src_ref=source,
            dst_ref=halo.at[step, field, 1 - side],
            send_sem=halo_send.at[step, field, side],
            recv_sem=halo_recv.at[step, field, 1 - side],
            device_id={"sub": lax.rem(me + sub_count - 1 + 2 * side, sub_count)},
            device_id_type=MESH,
        )

    def half_copy(half, side):
        step = step_count - 1
        return pltpu.make_async_remote_copy(
            src_ref=state.at[
                step,
                1,
                pl.ds(side * (span - REACH), REACH),
                pl.ds(halves[half] + MARGIN, half_rows),
                :,
            ],
            dst_ref=halo.at[step, 1, 1 - side, :, pl.ds(halves[half], half_rows), :],
            send_sem=half_send.at[half, side],
            recv_sem=half_recv.at[half, 1 - side],
            device_id={"sub": lax.rem(me + sub_count - 1 + 2 * side, sub_count)},
            device_id_type=MESH,
        )

    reaches = (has_before, has_after)

    def copies_of(step, field, side):
        if step == step_count - 1 and field == 1:
            return [half_copy(half, side) for half in range(2)]
        return [halo_copy(step, field, side)]

    def halo_start(step, field, side):
        @pl.when(reaches[side])
        def _():
            for copy in copies_of(step, field, side):
                copy.start()

    def halo_wait(step, field, side):
        @pl.when(reaches[side])
        def _():
            for copy in copies_of(step, field, 1 - side):
                copy.wait_recv()

    def half_wait(half, side):
        @pl.when(reaches[side])
        def _():
            half_copy(half, 1 - side).wait_recv()

    def halo_sent(step, field, side):
        @pl.when(reaches[side])
        def _():
            for copy in copies_of(step, field, side):
                copy.wait_send()

    pl.semaphore_wait(barrier, sub_count - 1 + shot_count - 1)


    for side in range(2):
        halo_start(0, 0, side)

    def clear_margins(index, carry):
        zero = jnp.zeros((MARGIN, cells_z), jnp.float32)
        for step in range(step_count):
            for field in range(2):
                state[step, field, index, pl.ds(0, MARGIN), :] = zero
                state[step, field, index, pl.ds(MARGIN + cells_y, MARGIN), :] = zero
        return carry

    lax.fori_loop(0, span, clear_margins, 0)

    def clear_halo(side):
        for step in range(step_count):
            for field in range(2):
                for plane in range(REACH):
                    halo[step, field, side, plane] = jnp.zeros((cells_y, cells_z), jnp.float32)

    @pl.when(jnp.logical_not(has_before))
    def _():
        clear_halo(0)

    @pl.when(jnp.logical_not(has_after))
    def _():
        clear_halo(1)

    apart = jnp.abs(iota((cells_z, cells_z), 0) - iota((cells_z, cells_z), 1))
    weights = jnp.where(apart == 0, 3.0 * STENCIL[0], 0.0)
    for offset in range(1, REACH + 1):
        weights = jnp.where(apart == offset, STENCIL[offset], weights)
    for column, weight in enumerate((rounded(weights), weights - rounded(weights))):
        for first in (0, cells_z):
            band[pl.ds(first, cells_z), pl.ds(column * cells_z, cells_z)] = weight.astype(
                jnp.bfloat16
            )

    for load in small_loads:
        load.wait()
    owner = owner_ref[...]
    cell = cell_ref[...]
    named = jnp.where(iota((sub_count, receivers), 0) == owner, 1.0, 0.0)
    earlier = onehot(iota((receivers, receivers), 0) < iota((receivers, receivers), 1))
    counts = jnp.dot(named.astype(jnp.bfloat16), earlier, preferred_element_type=jnp.float32)
    ranking = jnp.sum(counts * named, axis=0, keepdims=True).astype(jnp.int32)
    slot = owner * LANES + lax.rem(me, group) * capacity + ranking
    part = trace_ref[:, 0, :]
    width = step_count + 1
    terms[...] = jnp.zeros_like(terms)
    for third in range(3):
        high = rounded(part)
        terms[pl.ds(third * width, step_count), :] = high
        part = part - high
    terms[pl.ds(step_count, 1), :] = (lax.shift_right_logical(cell, 16) * 65536).astype(jnp.float32)
    terms[pl.ds(width + step_count, 1), :] = (
        jnp.bitwise_and(lax.shift_right_logical(cell, 8), 255) * 256
    ).astype(jnp.float32)
    terms[pl.ds(2 * width + step_count, 1), :] = jnp.bitwise_and(cell, 255).astype(jnp.float32)
    stacked = terms[...].astype(jnp.bfloat16)
    chunk = 4 * LANES
    for first in range(0, sub_count * LANES, chunk):
        picks = onehot(iota((chunk, receivers), 0) + first == slot)
        packed_terms[:, pl.ds(first, chunk)] = lax.dot_general(
            stacked, picks, NT, preferred_element_type=jnp.float32
        )
    for peer in range(sub_count):
        lanes = pl.ds(peer * LANES, LANES)
        packed[peer] = (
            packed_terms[pl.ds(0, width), lanes]
            + packed_terms[pl.ds(width, width), lanes]
            + packed_terms[pl.ds(2 * width, width), lanes]
        )

    swaps = []
    for offset in range(1, sub_count):
        peer = lax.rem(me + offset, sub_count)
        swaps.append(
            pltpu.make_async_remote_copy(
                src_ref=packed.at[peer],
                dst_ref=arrived.at[offset],
                send_sem=swap_send.at[offset],
                recv_sem=swap_recv.at[offset],
                device_id={"sub": peer},
                device_id_type=MESH,
            )
        )
    for swap in swaps:
        swap.start()
    for side in range(2):
        halo_start(0, 1, side)
    arrived[0] = packed[me]

    place = iota((SUBLANES, cells_z), 0) * cells_z + iota((SUBLANES, cells_z), 1)
    source_plane = source_x_ref[0, 0] - me * span
    source_place = source_yz_ref[0, 0]

    def put(step, field, plane, rows, value):
        if step == step_count - 1:
            final[field, 0, plane, rows, :] = value
        else:
            state[step + 1, field, plane, pl.ds(rows.start + MARGIN, rows.size), :] = value

    planes_at_once = 16

    def advance(step, field):
        def depth_part(index, carry):
            first = pl.multiple_of(index * planes_at_once, planes_at_once)
            value = state[step, field, pl.ds(first, planes_at_once), inside_y, :]
            value = value.reshape(planes_at_once * cells_y, cells_z)
            high = value.astype(jnp.bfloat16)
            low = (value - high.astype(jnp.float32)).astype(jnp.bfloat16)
            both = jnp.dot(
                jnp.concatenate([high, low], axis=1),
                band[...],
                preferred_element_type=jnp.float32,
            )
            total = both[:, :cells_z] + both[:, cells_z:]
            along[pl.ds(first, planes_at_once)] = total.reshape(planes_at_once, cells_y, cells_z)
            return carry

        lax.fori_loop(0, span // planes_at_once, depth_part, 0)

        def one_row(index, carry):
            first = pl.multiple_of(index * SUBLANES, SUBLANES)
            rows = pl.ds(first, SUBLANES)
            shifted = pl.ds(first + MARGIN, SUBLANES)
            column = [state[step, field, plane, shifted, :] for plane in range(span)]
            if field == 0:
                source_here = jnp.where(
                    place + first * cells_z == source_place, wavelet_ref[0, step], 0.0
                )
            for plane in range(span):
                total = along[plane, rows, :]
                for offset in range(1, REACH + 1):
                    near = (
                        state[step, field, plane, pl.ds(first + MARGIN + offset, SUBLANES), :]
                        + state[step, field, plane, pl.ds(first + MARGIN - offset, SUBLANES), :]
                    )
                    for other in (plane - offset, plane + offset):
                        if 0 <= other < span:
                            near = near + column[other]
                    total = total + STENCIL[offset] * near
                if step == 0:
                    past = later[field, plane, rows, :]
                else:
                    past = state[step - 1, field, plane, shifted, :]
                stepped = 2.0 * column[plane] - past + courant[plane, rows, :] * total
                if field == 0:
                    stepped = stepped - jnp.where(plane == source_plane, 1.0, 0.0) * source_here
                else:
                    stepped = stepped + inj[step, pl.ds(plane * cells_y + first, SUBLANES), :]
                put(step, field, plane, rows, stepped)
            return carry

        lax.fori_loop(0, cells_y // SUBLANES, one_row, 0)

    def add_halo(step, field, side, row=0, count=cells_y):
        base = side * (span - REACH)

        def one_row(index, carry):
            first = pl.multiple_of(row + index * SUBLANES, SUBLANES)
            rows = pl.ds(first, SUBLANES)
            shifted = pl.ds(first + MARGIN, SUBLANES)
            outside = [halo[step, field, side, plane, rows, :] for plane in range(REACH)]
            for plane in range(REACH):
                total = jnp.zeros((SUBLANES, cells_z), jnp.float32)
                for other in range(REACH):
                    distance = other + REACH - plane if side else plane + REACH - other
                    if distance <= REACH:
                        total = total + STENCIL[distance] * outside[other]
                if step == step_count - 1:
                    value = final[field, 0, base + plane, rows, :]
                else:
                    value = state[step + 1, field, base + plane, shifted, :]
                value = value + courant[base + plane, rows, :] * total
                put(step, field, base + plane, rows, value)
            return carry

        lax.fori_loop(0, count // SUBLANES, one_row, 0)

    def by_distance(near, far):
        even = lax.rem(me, 2) == 0
        for act, first, second in ((near, 1, 0), (far, 0, 1)):

            @pl.when(even)
            def _(act=act, side=first):
                act(side)

            @pl.when(jnp.logical_not(even))
            def _(act=act, side=second):
                act(side)

    loads[0].wait()
    loads[2].wait()
    loads[3].wait()
    advance(0, 0)

    slot_count = slots.shape[1]

    def receive():
        for swap in swaps:
            swap.wait_recv()
        for first in range(0, sub_count, group):
            joined = arrived[first]
            for other in range(1, group):
                joined = joined + arrived[first + other]
            slots[:, pl.ds(first // group * LANES, LANES)] = joined

    def deposit(step):
        here = slots[pl.ds(step_count, 1), :].astype(jnp.int32)
        row = here // cells_z
        depth = here - row * cells_z
        at_depth = iota((cells_z, slot_count), 0) == depth
        value = slots[pl.ds(step, 1), :]
        high = rounded(value)
        low = value - high
        spread[pl.ds(0, cells_z), :] = jnp.where(at_depth, high, 0.0).astype(jnp.bfloat16)
        spread[pl.ds(cells_z, cells_z), :] = jnp.where(at_depth, low, 0.0).astype(jnp.bfloat16)
        row_chunk = 512

        def one_chunk(index, carry):
            first = pl.multiple_of(index * row_chunk, row_chunk)
            rows = pl.ds(first, row_chunk)
            if step == 0:
                here = onehot(iota((row_chunk, slot_count), 0) + first == row)
                at_row[rows, :] = here
            else:
                here = at_row[rows, :]
            both = lax.dot_general(here, spread[...], NT, preferred_element_type=jnp.float32)
            inj[step, rows, :] = both[:, :cells_z] + both[:, cells_z:]
            return carry

        lax.fori_loop(0, span * cells_y // row_chunk, one_chunk, 0)

    aperture_here = aperture_ref[0, me].astype(jnp.float32)

    portions = (
        (REACH, span - 2 * REACH),
        (0, REACH),
        (span - REACH, REACH),
    )

    def image_planes(portion, row=0, rows=cells_y):
        first, count = portions[portion]
        within = pl.ds(row, rows)
        shifted = pl.ds(row + MARGIN, rows)

        def one_plane(index, carry):
            plane = index + first
            total = final[0, 0, plane, within, :] * final[1, 0, plane, within, :]
            for step in range(1, step_count):
                total = total + (
                    state[step, 0, plane, shifted, :] * state[step, 1, plane, shifted, :]
                )
            image[plane, within, :] = aperture_here * total
            return carry

        lax.fori_loop(0, count, one_plane, 0)

    def image_copies(portion, half):
        first, count = portions[portion]
        there = lax.rem(own_half + 1 - half, 2) * half_shots
        copies = []
        for turn in range(half, half_shots):
            peer = there + lax.rem(shot + turn, half_shots)
            slot = half * (half_shots - 1) + turn
            rows = pl.ds(pl.multiple_of(peer * own_rows, own_rows), own_rows)
            copies.append(
                pltpu.make_async_remote_copy(
                    src_ref=image.at[pl.ds(first, count), rows, :],
                    dst_ref=image_in.at[slot, pl.ds(first, count)],
                    send_sem=image_send.at[portion, slot],
                    recv_sem=image_recv.at[portion, slot],
                    device_id={"shot": peer},
                    device_id_type=MESH,
                )
            )
        return copies

    def image_start(portion, half):
        for copy in image_copies(portion, half):
            copy.start()

    def image_join(portion):
        first, count = portions[portion]
        for half in range(2):
            for copy in image_copies(portion, half):
                copy.wait_recv()
        rows = pl.ds(pl.multiple_of(shot * own_rows, own_rows), own_rows)

        def one_plane(index, carry):
            plane = index + first
            total = image[plane, rows, :]
            for slot in range(shot_count - 1):
                total = total + image_in[slot, plane]
            image_out[plane] = total
            return carry

        lax.fori_loop(0, count, one_plane, 0)

    last = step_count - 1

    def arrivals(step, field):
        def arrive(side):
            halo_wait(step, field, side)
            add_halo(step, field, side)
            if step < last:
                halo_start(step + 1, field, side)

        by_distance(arrive, arrive)

    for step in range(last):
        arrivals(step, 0)
        advance(step + 1, 0)
        if step == 0:
            receive()
            deposit(0)
            loads[1].wait()
            advance(0, 1)
        else:
            deposit(step + 1)
        arrivals(step, 1)
        if step == 0:
            deposit(1)
        advance(step + 1, 1)
    image_planes(0)
    for half in range(2):
        image_start(0, half)
    arrivals(last, 0)

    def near(side):
        halo_wait(last, 1, side)
        add_halo(last, 1, side)
        image_planes(1 + side)
        for half in range(2):
            image_start(1 + side, half)

    def far(side):
        for half in range(2):
            half_wait(half, side)
            add_halo(last, 1, side, halves[half], half_rows)
            image_planes(1 + side, halves[half], half_rows)
            image_start(1 + side, half)
            if half == 0:
                image_join(0)
                image_join(2 - side)
        image_join(1 + side)

    by_distance(near, far)
    for swap in swaps:
        swap.wait_send()
    for step in range(step_count):
        for field in range(2):
            for side in range(2):
                halo_sent(step, field, side)
    for portion in range(3):
        for half in range(2):
            for copy in image_copies(portion, half):
                copy.wait_send()


def local(
    courant,
    wave_now,
    wave_later,
    traces,
    rec_owner,
    rec_cell,
    source_x,
    source_yz,
    wavelet,
    aperture,
):
    span, cells_y, cells_z = courant.shape
    sub_count = lax.axis_size("sub")
    shot_count = lax.axis_size("shot")
    step_count, receivers = traces.shape[1:]
    capacity = max(2, 2 * receivers // sub_count)
    group = max(1, min(LANES // capacity, sub_count))
    slot_count = sub_count // group * LANES
    terms_height = -(-3 * (step_count + 1) // 16) * 16
    vmem = pl.BlockSpec(memory_space=pltpu.VMEM)
    hbm = pl.BlockSpec(memory_space=pl.ANY)
    dma = pltpu.SemaphoreType.DMA
    image, final = pl.pallas_call(
        functools.partial(kernel, sub_count, shot_count, step_count),
        out_shape=(
            pltpu.VMEM((span, cells_y // shot_count, cells_z), jnp.float32),
            pltpu.VMEM(wave_now.shape, jnp.float32),
        ),
        in_specs=[hbm] * 10,
        out_specs=(vmem, vmem),
        scratch_shapes=[
            pltpu.SMEM(wavelet.shape, jnp.float32),
            pltpu.SMEM((1, 1), jnp.int32),
            pltpu.SMEM((1, 1), jnp.int32),
            pltpu.SMEM(aperture.shape, jnp.int32),
            pltpu.VMEM((1, receivers), jnp.int32),
            pltpu.VMEM((1, receivers), jnp.int32),
            pltpu.VMEM((step_count, 1, receivers), jnp.float32),
            dma((7,)),
            pltpu.VMEM(
                (step_count, 2, span, cells_y + 2 * MARGIN, cells_z), jnp.float32
            ),
            pltpu.VMEM((step_count, 2, 2, REACH, cells_y, cells_z), jnp.float32),
            pltpu.VMEM((2 * cells_z, 2 * cells_z), jnp.bfloat16),
            pltpu.VMEM((span, cells_y, cells_z), jnp.float32),
            pltpu.VMEM((2, span, cells_y, cells_z), jnp.float32),
            pltpu.VMEM((span, cells_y, cells_z), jnp.float32),
            pltpu.VMEM((step_count, span * cells_y, cells_z), jnp.float32),
            pltpu.VMEM((span, cells_y, cells_z), jnp.float32),
            pltpu.VMEM(
                (max(1, shot_count - 1), span, cells_y // shot_count, cells_z), jnp.float32
            ),
            pltpu.VMEM((terms_height, receivers), jnp.float32),
            pltpu.VMEM((terms_height, sub_count * LANES), jnp.float32),
            pltpu.VMEM((sub_count, step_count + 1, LANES), jnp.float32),
            pltpu.VMEM((sub_count, step_count + 1, LANES), jnp.float32),
            pltpu.VMEM((step_count + 1, slot_count), jnp.float32),
            pltpu.VMEM((2 * cells_z, slot_count), jnp.bfloat16),
            pltpu.VMEM((span * cells_y, slot_count), jnp.bfloat16),
            dma((4,)),
            dma((step_count, 2, 2)),
            dma((step_count, 2, 2)),
            dma((2, 2)),
            dma((2, 2)),
            dma((sub_count,)),
            dma((sub_count,)),
            dma((3, max(1, shot_count - 1))),
            dma((3, max(1, shot_count - 1))),
        ],
        compiler_params=pltpu.CompilerParams(
            collective_id=0, has_side_effects=True
        ),
    )(
        wavelet,
        source_x.reshape(1, 1),
        source_yz.reshape(1, 1),
        aperture,
        rec_owner.reshape(1, receivers),
        rec_cell,
        jnp.transpose(traces, (1, 0, 2)),
        courant,
        wave_now,
        wave_later,
    )
    return image, final


def solution(mesh):
    in_specs = (
        P("sub", None, None),
        P(None, "shot", "sub", None, None),
        P(None, "shot", "sub", None, None),
        P("shot", None, "sub"),
        P("shot", "sub", None),
        P("shot", "sub"),
        P("shot"),
        P("shot"),
        P("shot", None),
        P("shot", None),
    )
    out_specs = (P("sub", "shot", None), P(None, "shot", "sub", None, None))
    return jax.shard_map(local, mesh=mesh, in_specs=in_specs, out_specs=out_specs, check_vma=False)
```

```python
import functools

import jax
import jax.numpy as jnp
from jax import lax
from jax.experimental import pallas as pl
from jax.experimental.pallas import tpu as pltpu
from jax.sharding import PartitionSpec as P

STENCIL = (-205.0 / 72.0, 8.0 / 5.0, -1.0 / 5.0, 8.0 / 315.0, -1.0 / 560.0)
REACH = len(STENCIL) - 1
MARGIN = 8
LANES = 128
SUBLANES = 8
MESH = pl.DeviceIdType.MESH
NT = (((1,), (1,)), ((), ()))


def iota(shape, dim):
    return lax.broadcasted_iota(jnp.int32, shape, dim)


def onehot(mask):
    return jnp.where(mask, 1.0, 0.0).astype(jnp.bfloat16)


def rounded(x):
    return x.astype(jnp.bfloat16).astype(jnp.float32)


def kernel(
    sub_count,
    shot_count,
    step_count,
    wavelet_hbm,
    source_x_hbm,
    source_yz_hbm,
    aperture_hbm,
    owner_hbm,
    cell_hbm,
    trace_hbm,
    courant_hbm,
    now_hbm,
    later_hbm,
    image_out,
    final,
    wavelet_ref,
    source_x_ref,
    source_yz_ref,
    aperture_ref,
    owner_ref,
    cell_ref,
    trace_ref,
    small_sem,
    state,
    halo,
    band,
    along,
    later,
    courant,
    inj,
    image,
    image_in,
    terms,
    packed_terms,
    packed,
    arrived,
    slots,
    spread,
    at_row,
    load_sem,
    halo_send,
    halo_recv,
    half_send,
    half_recv,
    swap_send,
    swap_recv,
    image_send,
    image_recv,
):
    span, cells_y, cells_z = courant.shape
    receivers = owner_ref.shape[1]
    capacity = max(2, 2 * receivers // sub_count)
    group = max(1, min(LANES // capacity, sub_count))
    own_rows = cells_y // shot_count
    me = lax.axis_index("sub")
    shot = lax.axis_index("shot")
    half_rows = cells_y // 2
    half_shots = shot_count // 2
    own_half = shot // half_shots
    halves = tuple(
        pl.multiple_of(half * half_rows, half_rows) for half in (1 - own_half, own_half)
    )
    has_before = me > 0
    has_after = me < sub_count - 1
    inside_y = pl.ds(MARGIN, cells_y)

    barrier = pltpu.get_barrier_semaphore()
    for offset in range(1, sub_count):
        pl.semaphore_signal(
            barrier,
            inc=1,
            device_id={"sub": lax.rem(me + offset, sub_count)},
            device_id_type=MESH,
        )
    for offset in range(1, shot_count):
        pl.semaphore_signal(
            barrier,
            inc=1,
            device_id={"shot": lax.rem(shot + offset, shot_count)},
            device_id_type=MESH,
        )

    small_loads = [
        pltpu.make_async_copy(source, target, small_sem.at[index])
        for index, (source, target) in enumerate(
            (
                (owner_hbm, owner_ref),
                (cell_hbm, cell_ref),
                (trace_hbm, trace_ref),
                (wavelet_hbm, wavelet_ref),
                (source_x_hbm, source_x_ref),
                (source_yz_hbm, source_yz_ref),
                (aperture_hbm, aperture_ref),
            )
        )
    ]
    for load in small_loads:
        load.start()
    loads = [
        pltpu.make_async_copy(
            now_hbm.at[field, 0],
            state.at[0, field, :, inside_y, :],
            load_sem.at[field],
        )
        for field in range(2)
    ]
    loads.append(pltpu.make_async_copy(later_hbm.at[:, 0], later, load_sem.at[2]))
    loads.append(pltpu.make_async_copy(courant_hbm, courant, load_sem.at[3]))
    for load in loads:
        load.start()

    def halo_copy(step, field, side):
        first = side * (span - REACH)
        if step == 0:
            source = now_hbm.at[field, 0, pl.ds(first, REACH)]
        else:
            source = state.at[step, field, pl.ds(first, REACH), inside_y, :]
        return pltpu.make_async_remote_copy(
            src_ref=source,
            dst_ref=halo.at[step, field, 1 - side],
            send_sem=halo_send.at[step, field, side],
            recv_sem=halo_recv.at[step, field, 1 - side],
            device_id={"sub": lax.rem(me + sub_count - 1 + 2 * side, sub_count)},
            device_id_type=MESH,
        )

    def half_copy(field, half, side):
        step = step_count - 1
        return pltpu.make_async_remote_copy(
            src_ref=state.at[
                step,
                field,
                pl.ds(side * (span - REACH), REACH),
                pl.ds(halves[half] + MARGIN, half_rows),
                :,
            ],
            dst_ref=halo.at[step, field, 1 - side, :, pl.ds(halves[half], half_rows), :],
            send_sem=half_send.at[field, half, side],
            recv_sem=half_recv.at[field, half, 1 - side],
            device_id={"sub": lax.rem(me + sub_count - 1 + 2 * side, sub_count)},
            device_id_type=MESH,
        )

    reaches = (has_before, has_after)

    def halo_start(step, field, side):
        @pl.when(reaches[side])
        def _():
            if step < step_count - 1:
                halo_copy(step, field, side).start()
            else:
                for other, half in ((0, 0),) if field == 0 else ((1, 0), (0, 1), (1, 1)):
                    half_copy(other, half, side).start()

    def halo_wait(step, field, side):
        @pl.when(reaches[side])
        def _():
            halo_copy(step, field, 1 - side).wait_recv()

    def half_wait(half, side):
        @pl.when(reaches[side])
        def _():
            for field in range(2):
                half_copy(field, half, 1 - side).wait_recv()

    def halo_sent(step, field, side):
        @pl.when(reaches[side])
        def _():
            if step < step_count - 1:
                halo_copy(step, field, side).wait_send()
            else:
                for half in range(2):
                    half_copy(field, half, side).wait_send()

    pl.semaphore_wait(barrier, sub_count - 1 + shot_count - 1)


    for side in range(2):
        halo_start(0, 0, side)

    def clear_margins(index, carry):
        zero = jnp.zeros((MARGIN, cells_z), jnp.float32)
        for step in range(step_count):
            for field in range(2):
                state[step, field, index, pl.ds(0, MARGIN), :] = zero
                state[step, field, index, pl.ds(MARGIN + cells_y, MARGIN), :] = zero
        return carry

    lax.fori_loop(0, span, clear_margins, 0)

    def clear_halo(side):
        for step in range(step_count):
            for field in range(2):
                for plane in range(REACH):
                    halo[step, field, side, plane] = jnp.zeros((cells_y, cells_z), jnp.float32)

    @pl.when(jnp.logical_not(has_before))
    def _():
        clear_halo(0)

    @pl.when(jnp.logical_not(has_after))
    def _():
        clear_halo(1)

    apart = jnp.abs(iota((cells_z, cells_z), 0) - iota((cells_z, cells_z), 1))
    weights = jnp.where(apart == 0, 3.0 * STENCIL[0], 0.0)
    for offset in range(1, REACH + 1):
        weights = jnp.where(apart == offset, STENCIL[offset], weights)
    for column, weight in enumerate((rounded(weights), weights - rounded(weights))):
        for first in (0, cells_z):
            band[pl.ds(first, cells_z), pl.ds(column * cells_z, cells_z)] = weight.astype(
                jnp.bfloat16
            )

    for load in small_loads:
        load.wait()
    owner = owner_ref[...]
    cell = cell_ref[...]
    named = jnp.where(iota((sub_count, receivers), 0) == owner, 1.0, 0.0)
    earlier = onehot(iota((receivers, receivers), 0) < iota((receivers, receivers), 1))
    counts = jnp.dot(named.astype(jnp.bfloat16), earlier, preferred_element_type=jnp.float32)
    ranking = jnp.sum(counts * named, axis=0, keepdims=True).astype(jnp.int32)
    slot = owner * LANES + lax.rem(me, group) * capacity + ranking
    part = trace_ref[:, 0, :]
    width = step_count + 1
    terms[...] = jnp.zeros_like(terms)
    for third in range(3):
        high = rounded(part)
        terms[pl.ds(third * width, step_count), :] = high
        part = part - high
    terms[pl.ds(step_count, 1), :] = (lax.shift_right_logical(cell, 16) * 65536).astype(jnp.float32)
    terms[pl.ds(width + step_count, 1), :] = (
        jnp.bitwise_and(lax.shift_right_logical(cell, 8), 255) * 256
    ).astype(jnp.float32)
    terms[pl.ds(2 * width + step_count, 1), :] = jnp.bitwise_and(cell, 255).astype(jnp.float32)
    stacked = terms[...].astype(jnp.bfloat16)
    chunk = 4 * LANES
    for first in range(0, sub_count * LANES, chunk):
        picks = onehot(iota((chunk, receivers), 0) + first == slot)
        packed_terms[:, pl.ds(first, chunk)] = lax.dot_general(
            stacked, picks, NT, preferred_element_type=jnp.float32
        )
    for peer in range(sub_count):
        lanes = pl.ds(peer * LANES, LANES)
        packed[peer] = (
            packed_terms[pl.ds(0, width), lanes]
            + packed_terms[pl.ds(width, width), lanes]
            + packed_terms[pl.ds(2 * width, width), lanes]
        )

    swaps = []
    for offset in range(1, sub_count):
        peer = lax.rem(me + offset, sub_count)
        swaps.append(
            pltpu.make_async_remote_copy(
                src_ref=packed.at[peer],
                dst_ref=arrived.at[offset],
                send_sem=swap_send.at[offset],
                recv_sem=swap_recv.at[offset],
                device_id={"sub": peer},
                device_id_type=MESH,
            )
        )
    for swap in swaps:
        swap.start()
    for side in range(2):
        halo_start(0, 1, side)
    arrived[0] = packed[me]

    place = iota((SUBLANES, cells_z), 0) * cells_z + iota((SUBLANES, cells_z), 1)
    source_plane = source_x_ref[0, 0] - me * span
    source_place = source_yz_ref[0, 0]

    def put(step, field, plane, rows, value):
        if step == step_count - 1:
            final[field, 0, plane, rows, :] = value
        else:
            state[step + 1, field, plane, pl.ds(rows.start + MARGIN, rows.size), :] = value

    planes_at_once = 16

    def along_depth(step, field):
        def depth_part(index, carry):
            first = pl.multiple_of(index * planes_at_once, planes_at_once)
            value = state[step, field, pl.ds(first, planes_at_once), inside_y, :]
            value = value.reshape(planes_at_once * cells_y, cells_z)
            high = value.astype(jnp.bfloat16)
            low = (value - high.astype(jnp.float32)).astype(jnp.bfloat16)
            both = jnp.dot(
                jnp.concatenate([high, low], axis=1),
                band[...],
                preferred_element_type=jnp.float32,
            )
            total = both[:, :cells_z] + both[:, cells_z:]
            along[pl.ds(first, planes_at_once)] = total.reshape(planes_at_once, cells_y, cells_z)
            return carry

        lax.fori_loop(0, span // planes_at_once, depth_part, 0)

    def advance_rows(step, field, row, count):
        def one_row(index, carry):
            first = pl.multiple_of(row + index * SUBLANES, SUBLANES)
            rows = pl.ds(first, SUBLANES)
            shifted = pl.ds(first + MARGIN, SUBLANES)
            column = [state[step, field, plane, shifted, :] for plane in range(span)]
            if field == 0:
                source_here = jnp.where(
                    place + first * cells_z == source_place, wavelet_ref[0, step], 0.0
                )
            for plane in range(span):
                total = along[plane, rows, :]
                for offset in range(1, REACH + 1):
                    near = (
                        state[step, field, plane, pl.ds(first + MARGIN + offset, SUBLANES), :]
                        + state[step, field, plane, pl.ds(first + MARGIN - offset, SUBLANES), :]
                    )
                    for other in (plane - offset, plane + offset):
                        if 0 <= other < span:
                            near = near + column[other]
                    total = total + STENCIL[offset] * near
                if step == 0:
                    past = later[field, plane, rows, :]
                else:
                    past = state[step - 1, field, plane, shifted, :]
                stepped = 2.0 * column[plane] - past + courant[plane, rows, :] * total
                if field == 0:
                    stepped = stepped - jnp.where(plane == source_plane, 1.0, 0.0) * source_here
                else:
                    stepped = stepped + inj[step, pl.ds(plane * cells_y + first, SUBLANES), :]
                put(step, field, plane, rows, stepped)
            return carry

        lax.fori_loop(0, count // SUBLANES, one_row, 0)

    def advance(step, field):
        along_depth(step, field)
        advance_rows(step, field, 0, cells_y)

    def add_halo(step, field, side, row=0, count=cells_y):
        base = side * (span - REACH)

        def one_row(index, carry):
            first = pl.multiple_of(row + index * SUBLANES, SUBLANES)
            rows = pl.ds(first, SUBLANES)
            shifted = pl.ds(first + MARGIN, SUBLANES)
            outside = [halo[step, field, side, plane, rows, :] for plane in range(REACH)]
            for plane in range(REACH):
                total = jnp.zeros((SUBLANES, cells_z), jnp.float32)
                for other in range(REACH):
                    distance = other + REACH - plane if side else plane + REACH - other
                    if distance <= REACH:
                        total = total + STENCIL[distance] * outside[other]
                if step == step_count - 1:
                    value = final[field, 0, base + plane, rows, :]
                else:
                    value = state[step + 1, field, base + plane, shifted, :]
                value = value + courant[base + plane, rows, :] * total
                put(step, field, base + plane, rows, value)
            return carry

        lax.fori_loop(0, count // SUBLANES, one_row, 0)

    def by_distance(near, far):
        even = lax.rem(me, 2) == 0
        for act, first, second in ((near, 1, 0), (far, 0, 1)):

            @pl.when(even)
            def _(act=act, side=first):
                act(side)

            @pl.when(jnp.logical_not(even))
            def _(act=act, side=second):
                act(side)

    loads[0].wait()
    loads[2].wait()
    loads[3].wait()
    advance(0, 0)

    slot_count = slots.shape[1]

    def receive():
        for swap in swaps:
            swap.wait_recv()
        for first in range(0, sub_count, group):
            joined = arrived[first]
            for other in range(1, group):
                joined = joined + arrived[first + other]
            slots[:, pl.ds(first // group * LANES, LANES)] = joined

    def deposit(step):
        here = slots[pl.ds(step_count, 1), :].astype(jnp.int32)
        row = here // cells_z
        depth = here - row * cells_z
        at_depth = iota((cells_z, slot_count), 0) == depth
        value = slots[pl.ds(step, 1), :]
        high = rounded(value)
        low = value - high
        spread[pl.ds(0, cells_z), :] = jnp.where(at_depth, high, 0.0).astype(jnp.bfloat16)
        spread[pl.ds(cells_z, cells_z), :] = jnp.where(at_depth, low, 0.0).astype(jnp.bfloat16)
        row_chunk = 512

        def one_chunk(index, carry):
            first = pl.multiple_of(index * row_chunk, row_chunk)
            rows = pl.ds(first, row_chunk)
            if step == 0:
                here = onehot(iota((row_chunk, slot_count), 0) + first == row)
                at_row[rows, :] = here
            else:
                here = at_row[rows, :]
            both = lax.dot_general(here, spread[...], NT, preferred_element_type=jnp.float32)
            inj[step, rows, :] = both[:, :cells_z] + both[:, cells_z:]
            return carry

        lax.fori_loop(0, span * cells_y // row_chunk, one_chunk, 0)

    aperture_here = aperture_ref[0, me].astype(jnp.float32)

    portions = (
        (REACH, span - 2 * REACH),
        (0, REACH),
        (span - REACH, REACH),
    )

    def image_planes(portion, row=0, rows=cells_y):
        first, count = portions[portion]
        within = pl.ds(row, rows)
        shifted = pl.ds(row + MARGIN, rows)

        def one_plane(index, carry):
            plane = index + first
            total = final[0, 0, plane, within, :] * final[1, 0, plane, within, :]
            for step in range(1, step_count):
                total = total + (
                    state[step, 0, plane, shifted, :] * state[step, 1, plane, shifted, :]
                )
            image[plane, within, :] = aperture_here * total
            return carry

        lax.fori_loop(0, count, one_plane, 0)

    def image_copies(portion, half):
        first, count = portions[portion]
        there = lax.rem(own_half + 1 - half, 2) * half_shots
        copies = []
        for turn in range(half, half_shots):
            peer = there + lax.rem(shot + turn, half_shots)
            slot = half * (half_shots - 1) + turn
            rows = pl.ds(pl.multiple_of(peer * own_rows, own_rows), own_rows)
            copies.append(
                pltpu.make_async_remote_copy(
                    src_ref=image.at[pl.ds(first, count), rows, :],
                    dst_ref=image_in.at[slot, pl.ds(first, count)],
                    send_sem=image_send.at[portion, slot],
                    recv_sem=image_recv.at[portion, slot],
                    device_id={"shot": peer},
                    device_id_type=MESH,
                )
            )
        return copies

    def image_start(portion, half):
        for copy in image_copies(portion, half):
            copy.start()

    def image_join(portion):
        first, count = portions[portion]
        for half in range(2):
            for copy in image_copies(portion, half):
                copy.wait_recv()
        rows = pl.ds(pl.multiple_of(shot * own_rows, own_rows), own_rows)

        def one_plane(index, carry):
            plane = index + first
            total = image[plane, rows, :]
            for slot in range(shot_count - 1):
                total = total + image_in[slot, plane]
            image_out[plane] = total
            return carry

        lax.fori_loop(0, count, one_plane, 0)

    last = step_count - 1

    def arrivals(step, field):
        def arrive(side):
            halo_wait(step, field, side)
            add_halo(step, field, side)
            if step < last:
                halo_start(step + 1, field, side)

        by_distance(arrive, arrive)

    for step in range(last):
        arrivals(step, 0)
        advance(step + 1, 0)
        if step == 0:
            receive()
            deposit(0)
            loads[1].wait()
            advance(0, 1)
        else:
            deposit(step + 1)
        arrivals(step, 1)
        if step == 0:
            deposit(1)
        if step + 1 < last:
            advance(step + 1, 1)

    along_depth(last, 1)
    for half in range(2):
        advance_rows(last, 1, halves[half], half_rows)
        if half == 0:
            image_planes(0, halves[0], half_rows)
            image_start(0, 0)

    def finish(half, side):
        half_wait(half, side)
        for field in range(2):
            add_halo(last, field, side, halves[half], half_rows)
        image_planes(1 + side, halves[half], half_rows)
        image_start(1 + side, half)

    def near(side):
        for half in range(2):
            finish(half, side)
        image_planes(0, halves[1], half_rows)
        image_start(0, 1)

    def far(side):
        finish(0, side)
        image_join(0)
        finish(1, side)
        for portion in (2 - side, 1 + side):
            image_join(portion)

    by_distance(near, far)
    for swap in swaps:
        swap.wait_send()
    for step in range(step_count):
        for field in range(2):
            for side in range(2):
                halo_sent(step, field, side)
    for portion in range(3):
        for half in range(2):
            for copy in image_copies(portion, half):
                copy.wait_send()


def write_out(image_ref, final_ref, image_hbm, final_hbm, sem):
    copies = [
        pltpu.make_async_copy(source, target, sem.at[index])
        for index, (source, target) in enumerate(
            ((final_ref, final_hbm), (image_ref, image_hbm))
        )
    ]
    for copy in copies:
        copy.start()
    for copy in copies:
        copy.wait()


def local(
    courant,
    wave_now,
    wave_later,
    traces,
    rec_owner,
    rec_cell,
    source_x,
    source_yz,
    wavelet,
    aperture,
):
    span, cells_y, cells_z = courant.shape
    sub_count = lax.axis_size("sub")
    shot_count = lax.axis_size("shot")
    step_count, receivers = traces.shape[1:]
    capacity = max(2, 2 * receivers // sub_count)
    group = max(1, min(LANES // capacity, sub_count))
    slot_count = sub_count // group * LANES
    terms_height = -(-3 * (step_count + 1) // 16) * 16
    vmem = pl.BlockSpec(memory_space=pltpu.VMEM)
    hbm = pl.BlockSpec(memory_space=pl.ANY)
    dma = pltpu.SemaphoreType.DMA
    image, final = pl.pallas_call(
        functools.partial(kernel, sub_count, shot_count, step_count),
        out_shape=(
            pltpu.VMEM((span, cells_y // shot_count, cells_z), jnp.float32),
            pltpu.VMEM(wave_now.shape, jnp.float32),
        ),
        in_specs=[hbm] * 10,
        out_specs=(vmem, vmem),
        scratch_shapes=[
            pltpu.SMEM(wavelet.shape, jnp.float32),
            pltpu.SMEM((1, 1), jnp.int32),
            pltpu.SMEM((1, 1), jnp.int32),
            pltpu.SMEM(aperture.shape, jnp.int32),
            pltpu.VMEM((1, receivers), jnp.int32),
            pltpu.VMEM((1, receivers), jnp.int32),
            pltpu.VMEM((step_count, 1, receivers), jnp.float32),
            dma((7,)),
            pltpu.VMEM(
                (step_count, 2, span, cells_y + 2 * MARGIN, cells_z), jnp.float32
            ),
            pltpu.VMEM((step_count, 2, 2, REACH, cells_y, cells_z), jnp.float32),
            pltpu.VMEM((2 * cells_z, 2 * cells_z), jnp.bfloat16),
            pltpu.VMEM((span, cells_y, cells_z), jnp.float32),
            pltpu.VMEM((2, span, cells_y, cells_z), jnp.float32),
            pltpu.VMEM((span, cells_y, cells_z), jnp.float32),
            pltpu.VMEM((step_count, span * cells_y, cells_z), jnp.float32),
            pltpu.VMEM((span, cells_y, cells_z), jnp.float32),
            pltpu.VMEM(
                (max(1, shot_count - 1), span, cells_y // shot_count, cells_z), jnp.float32
            ),
            pltpu.VMEM((terms_height, receivers), jnp.float32),
            pltpu.VMEM((terms_height, sub_count * LANES), jnp.float32),
            pltpu.VMEM((sub_count, step_count + 1, LANES), jnp.float32),
            pltpu.VMEM((sub_count, step_count + 1, LANES), jnp.float32),
            pltpu.VMEM((step_count + 1, slot_count), jnp.float32),
            pltpu.VMEM((2 * cells_z, slot_count), jnp.bfloat16),
            pltpu.VMEM((span * cells_y, slot_count), jnp.bfloat16),
            dma((4,)),
            dma((step_count, 2, 2)),
            dma((step_count, 2, 2)),
            dma((2, 2, 2)),
            dma((2, 2, 2)),
            dma((sub_count,)),
            dma((sub_count,)),
            dma((3, max(1, shot_count - 1))),
            dma((3, max(1, shot_count - 1))),
        ],
        compiler_params=pltpu.CompilerParams(
            collective_id=0, has_side_effects=True
        ),
    )(
        wavelet,
        source_x.reshape(1, 1),
        source_yz.reshape(1, 1),
        aperture,
        rec_owner.reshape(1, receivers),
        rec_cell,
        jnp.transpose(traces, (1, 0, 2)),
        courant,
        wave_now,
        wave_later,
    )
    return pl.pallas_call(
        write_out,
        out_shape=(
            jax.ShapeDtypeStruct(image.shape, jnp.float32),
            jax.ShapeDtypeStruct(final.shape, jnp.float32),
        ),
        in_specs=[vmem, vmem],
        out_specs=(hbm, hbm),
        scratch_shapes=[dma((2,))],
    )(
        pltpu.with_memory_space_constraint(image, pltpu.VMEM),
        pltpu.with_memory_space_constraint(final, pltpu.VMEM),
    )


def solution(mesh):
    in_specs = (
        P("sub", None, None),
        P(None, "shot", "sub", None, None),
        P(None, "shot", "sub", None, None),
        P("shot", None, "sub"),
        P("shot", "sub", None),
        P("shot", "sub"),
        P("shot"),
        P("shot"),
        P("shot", None),
        P("shot", None),
    )
    out_specs = (P("sub", "shot", None), P(None, "shot", "sub", None, None))
    return jax.shard_map(local, mesh=mesh, in_specs=in_specs, out_specs=out_specs, check_vma=False)
```

```python
import functools

import jax
import jax.numpy as jnp
from jax import lax
from jax.experimental import pallas as pl
from jax.experimental.pallas import tpu as pltpu
from jax.sharding import PartitionSpec as P

STENCIL = (-205.0 / 72.0, 8.0 / 5.0, -1.0 / 5.0, 8.0 / 315.0, -1.0 / 560.0)
REACH = len(STENCIL) - 1
MARGIN = 8
LANES = 128
SUBLANES = 8
MESH = pl.DeviceIdType.MESH
NT = (((1,), (1,)), ((), ()))


def iota(shape, dim):
    return lax.broadcasted_iota(jnp.int32, shape, dim)


def onehot(mask):
    return jnp.where(mask, 1.0, 0.0).astype(jnp.bfloat16)


def rounded(x):
    return x.astype(jnp.bfloat16).astype(jnp.float32)


def kernel(
    sub_count,
    shot_count,
    step_count,
    wavelet_hbm,
    source_x_hbm,
    source_yz_hbm,
    aperture_hbm,
    owner_hbm,
    cell_hbm,
    trace_hbm,
    courant_hbm,
    now_hbm,
    later_hbm,
    image_out,
    final,
    wavelet_ref,
    source_x_ref,
    source_yz_ref,
    aperture_ref,
    owner_ref,
    cell_ref,
    trace_ref,
    small_sem,
    state,
    halo,
    band,
    along,
    later,
    courant,
    inj,
    image,
    image_in,
    terms,
    packed_terms,
    packed,
    arrived,
    slots,
    spread,
    at_row,
    load_sem,
    halo_send,
    halo_recv,
    half_send,
    half_recv,
    swap_send,
    swap_recv,
    image_send,
    image_recv,
):
    span, cells_y, cells_z = courant.shape
    receivers = owner_ref.shape[1]
    capacity = max(2, 2 * receivers // sub_count)
    group = max(1, min(LANES // capacity, sub_count))
    own_rows = cells_y // shot_count
    me = lax.axis_index("sub")
    shot = lax.axis_index("shot")
    half_rows = cells_y // 2
    half_shots = shot_count // 2
    own_half = shot // half_shots
    halves = tuple(
        pl.multiple_of(half * half_rows, half_rows) for half in (1 - own_half, own_half)
    )
    has_before = me > 0
    has_after = me < sub_count - 1
    inside_y = pl.ds(MARGIN, cells_y)

    barrier = pltpu.get_barrier_semaphore()
    for offset in range(1, sub_count):
        pl.semaphore_signal(
            barrier,
            inc=1,
            device_id={"sub": lax.rem(me + offset, sub_count)},
            device_id_type=MESH,
        )
    for offset in range(1, shot_count):
        pl.semaphore_signal(
            barrier,
            inc=1,
            device_id={"shot": lax.rem(shot + offset, shot_count)},
            device_id_type=MESH,
        )

    small_loads = [
        pltpu.make_async_copy(source, target, small_sem.at[index])
        for index, (source, target) in enumerate(
            (
                (owner_hbm, owner_ref),
                (cell_hbm, cell_ref),
                (trace_hbm, trace_ref),
                (wavelet_hbm, wavelet_ref),
                (source_x_hbm, source_x_ref),
                (source_yz_hbm, source_yz_ref),
                (aperture_hbm, aperture_ref),
            )
        )
    ]
    for load in small_loads:
        load.start()
    loads = [
        pltpu.make_async_copy(
            now_hbm.at[field, 0],
            state.at[0, field, :, inside_y, :],
            load_sem.at[field],
        )
        for field in range(2)
    ]
    loads.append(pltpu.make_async_copy(later_hbm.at[:, 0], later, load_sem.at[2]))
    loads.append(pltpu.make_async_copy(courant_hbm, courant, load_sem.at[3]))
    for load in loads:
        load.start()

    def halo_copy(step, field, side):
        first = side * (span - REACH)
        if step == 0:
            source = now_hbm.at[field, 0, pl.ds(first, REACH)]
        else:
            source = state.at[step, field, pl.ds(first, REACH), inside_y, :]
        return pltpu.make_async_remote_copy(
            src_ref=source,
            dst_ref=halo.at[step, field, 1 - side],
            send_sem=halo_send.at[step, field, side],
            recv_sem=halo_recv.at[step, field, 1 - side],
            device_id={"sub": lax.rem(me + sub_count - 1 + 2 * side, sub_count)},
            device_id_type=MESH,
        )

    def half_copy(field, half, side):
        step = step_count - 1
        return pltpu.make_async_remote_copy(
            src_ref=state.at[
                step,
                field,
                pl.ds(side * (span - REACH), REACH),
                pl.ds(halves[half] + MARGIN, half_rows),
                :,
            ],
            dst_ref=halo.at[step, field, 1 - side, :, pl.ds(halves[half], half_rows), :],
            send_sem=half_send.at[field, half, side],
            recv_sem=half_recv.at[field, half, 1 - side],
            device_id={"sub": lax.rem(me + sub_count - 1 + 2 * side, sub_count)},
            device_id_type=MESH,
        )

    reaches = (has_before, has_after)

    def halo_start(step, field, side):
        @pl.when(reaches[side])
        def _():
            if step < step_count - 1:
                halo_copy(step, field, side).start()
            else:
                for other, half in ((0, 0),) if field == 0 else ((1, 0), (0, 1), (1, 1)):
                    half_copy(other, half, side).start()

    def halo_wait(step, field, side):
        @pl.when(reaches[side])
        def _():
            halo_copy(step, field, 1 - side).wait_recv()

    def half_wait(half, side):
        @pl.when(reaches[side])
        def _():
            for field in range(2):
                half_copy(field, half, 1 - side).wait_recv()

    def halo_sent(step, field, side):
        @pl.when(reaches[side])
        def _():
            if step < step_count - 1:
                halo_copy(step, field, side).wait_send()
            else:
                for half in range(2):
                    half_copy(field, half, side).wait_send()

    pl.semaphore_wait(barrier, sub_count - 1 + shot_count - 1)


    for side in range(2):
        halo_start(0, 0, side)

    def clear_margins(index, carry):
        zero = jnp.zeros((MARGIN, cells_z), jnp.float32)
        for step in range(step_count):
            for field in range(2):
                state[step, field, index, pl.ds(0, MARGIN), :] = zero
                state[step, field, index, pl.ds(MARGIN + cells_y, MARGIN), :] = zero
        return carry

    lax.fori_loop(0, span, clear_margins, 0)

    def clear_halo(side):
        for step in range(step_count):
            for field in range(2):
                for plane in range(REACH):
                    halo[step, field, side, plane] = jnp.zeros((cells_y, cells_z), jnp.float32)

    @pl.when(jnp.logical_not(has_before))
    def _():
        clear_halo(0)

    @pl.when(jnp.logical_not(has_after))
    def _():
        clear_halo(1)

    apart = jnp.abs(iota((cells_z, cells_z), 0) - iota((cells_z, cells_z), 1))
    weights = jnp.where(apart == 0, 3.0 * STENCIL[0], 0.0)
    for offset in range(1, REACH + 1):
        weights = jnp.where(apart == offset, STENCIL[offset], weights)
    for column, weight in enumerate((rounded(weights), weights - rounded(weights))):
        for first in (0, cells_z):
            band[pl.ds(first, cells_z), pl.ds(column * cells_z, cells_z)] = weight.astype(
                jnp.bfloat16
            )

    for load in small_loads:
        load.wait()
    owner = owner_ref[...]
    cell = cell_ref[...]
    named = jnp.where(iota((sub_count, receivers), 0) == owner, 1.0, 0.0)
    earlier = onehot(iota((receivers, receivers), 0) < iota((receivers, receivers), 1))
    counts = jnp.dot(named.astype(jnp.bfloat16), earlier, preferred_element_type=jnp.float32)
    ranking = jnp.sum(counts * named, axis=0, keepdims=True).astype(jnp.int32)
    slot = owner * LANES + lax.rem(me, group) * capacity + ranking
    part = trace_ref[:, 0, :]
    width = step_count + 1
    terms[...] = jnp.zeros_like(terms)
    for third in range(3):
        high = rounded(part)
        terms[pl.ds(third * width, step_count), :] = high
        part = part - high
    terms[pl.ds(step_count, 1), :] = (lax.shift_right_logical(cell, 16) * 65536).astype(jnp.float32)
    terms[pl.ds(width + step_count, 1), :] = (
        jnp.bitwise_and(lax.shift_right_logical(cell, 8), 255) * 256
    ).astype(jnp.float32)
    terms[pl.ds(2 * width + step_count, 1), :] = jnp.bitwise_and(cell, 255).astype(jnp.float32)
    stacked = terms[...].astype(jnp.bfloat16)
    chunk = 4 * LANES
    for first in range(0, sub_count * LANES, chunk):
        picks = onehot(iota((chunk, receivers), 0) + first == slot)
        packed_terms[:, pl.ds(first, chunk)] = lax.dot_general(
            stacked, picks, NT, preferred_element_type=jnp.float32
        )
    for peer in range(sub_count):
        lanes = pl.ds(peer * LANES, LANES)
        packed[peer] = (
            packed_terms[pl.ds(0, width), lanes]
            + packed_terms[pl.ds(width, width), lanes]
            + packed_terms[pl.ds(2 * width, width), lanes]
        )

    swaps = []
    for offset in range(1, sub_count):
        peer = lax.rem(me + offset, sub_count)
        swaps.append(
            pltpu.make_async_remote_copy(
                src_ref=packed.at[peer],
                dst_ref=arrived.at[offset],
                send_sem=swap_send.at[offset],
                recv_sem=swap_recv.at[offset],
                device_id={"sub": peer},
                device_id_type=MESH,
            )
        )
    for swap in swaps:
        swap.start()
    for side in range(2):
        halo_start(0, 1, side)
    arrived[0] = packed[me]

    place = iota((SUBLANES, cells_z), 0) * cells_z + iota((SUBLANES, cells_z), 1)
    source_plane = source_x_ref[0, 0] - me * span
    source_place = source_yz_ref[0, 0]

    def put(step, field, plane, rows, value):
        if step == step_count - 1:
            final[field, 0, plane, rows, :] = value
        else:
            state[step + 1, field, plane, pl.ds(rows.start + MARGIN, rows.size), :] = value

    planes_at_once = 16

    def along_depth(step, field):
        def depth_part(index, carry):
            first = pl.multiple_of(index * planes_at_once, planes_at_once)
            value = state[step, field, pl.ds(first, planes_at_once), inside_y, :]
            value = value.reshape(planes_at_once * cells_y, cells_z)
            high = value.astype(jnp.bfloat16)
            low = (value - high.astype(jnp.float32)).astype(jnp.bfloat16)
            both = jnp.dot(
                jnp.concatenate([high, low], axis=1),
                band[...],
                preferred_element_type=jnp.float32,
            )
            total = both[:, :cells_z] + both[:, cells_z:]
            along[pl.ds(first, planes_at_once)] = total.reshape(planes_at_once, cells_y, cells_z)
            return carry

        lax.fori_loop(0, span // planes_at_once, depth_part, 0)

    def advance_rows(step, field, row, count):
        def one_row(index, carry):
            first = pl.multiple_of(row + index * SUBLANES, SUBLANES)
            rows = pl.ds(first, SUBLANES)
            shifted = pl.ds(first + MARGIN, SUBLANES)
            column = [state[step, field, plane, shifted, :] for plane in range(span)]
            if field == 0:
                source_here = jnp.where(
                    place + first * cells_z == source_place, wavelet_ref[0, step], 0.0
                )
            for plane in range(span):
                total = along[plane, rows, :]
                for offset in range(1, REACH + 1):
                    near = (
                        state[step, field, plane, pl.ds(first + MARGIN + offset, SUBLANES), :]
                        + state[step, field, plane, pl.ds(first + MARGIN - offset, SUBLANES), :]
                    )
                    for other in (plane - offset, plane + offset):
                        if 0 <= other < span:
                            near = near + column[other]
                    total = total + STENCIL[offset] * near
                if step == 0:
                    past = later[field, plane, rows, :]
                else:
                    past = state[step - 1, field, plane, shifted, :]
                stepped = 2.0 * column[plane] - past + courant[plane, rows, :] * total
                if field == 0:
                    stepped = stepped - jnp.where(plane == source_plane, 1.0, 0.0) * source_here
                elif step > 0:
                    stepped = stepped + inj[step, pl.ds(plane * cells_y + first, SUBLANES), :]
                put(step, field, plane, rows, stepped)
            return carry

        lax.fori_loop(0, count // SUBLANES, one_row, 0)

    def advance(step, field):
        along_depth(step, field)
        advance_rows(step, field, 0, cells_y)

    def add_halo(step, field, side, row=0, count=cells_y):
        base = side * (span - REACH)

        def one_row(index, carry):
            first = pl.multiple_of(row + index * SUBLANES, SUBLANES)
            rows = pl.ds(first, SUBLANES)
            shifted = pl.ds(first + MARGIN, SUBLANES)
            outside = [halo[step, field, side, plane, rows, :] for plane in range(REACH)]
            for plane in range(REACH):
                total = jnp.zeros((SUBLANES, cells_z), jnp.float32)
                for other in range(REACH):
                    distance = other + REACH - plane if side else plane + REACH - other
                    if distance <= REACH:
                        total = total + STENCIL[distance] * outside[other]
                if step == step_count - 1:
                    value = final[field, 0, base + plane, rows, :]
                else:
                    value = state[step + 1, field, base + plane, shifted, :]
                value = value + courant[base + plane, rows, :] * total
                put(step, field, base + plane, rows, value)
            return carry

        lax.fori_loop(0, count // SUBLANES, one_row, 0)

    def by_distance(near, far):
        even = lax.rem(me, 2) == 0
        for act, first, second in ((near, 1, 0), (far, 0, 1)):

            @pl.when(even)
            def _(act=act, side=first):
                act(side)

            @pl.when(jnp.logical_not(even))
            def _(act=act, side=second):
                act(side)

    loads[0].wait()
    loads[2].wait()
    loads[3].wait()
    advance(0, 0)
    loads[1].wait()
    advance(0, 1)

    slot_count = slots.shape[1]

    def receive():
        for swap in swaps:
            swap.wait_recv()
        for first in range(0, sub_count, group):
            joined = arrived[first]
            for other in range(1, group):
                joined = joined + arrived[first + other]
            slots[:, pl.ds(first // group * LANES, LANES)] = joined

    def deposit(step):
        here = slots[pl.ds(step_count, 1), :].astype(jnp.int32)
        row = here // cells_z
        depth = here - row * cells_z
        at_depth = iota((cells_z, slot_count), 0) == depth
        value = slots[pl.ds(step, 1), :]
        high = rounded(value)
        low = value - high
        spread[pl.ds(0, cells_z), :] = jnp.where(at_depth, high, 0.0).astype(jnp.bfloat16)
        spread[pl.ds(cells_z, cells_z), :] = jnp.where(at_depth, low, 0.0).astype(jnp.bfloat16)
        row_chunk = 512

        def one_chunk(index, carry):
            first = pl.multiple_of(index * row_chunk, row_chunk)
            rows = pl.ds(first, row_chunk)
            if step == 0:
                here = onehot(iota((row_chunk, slot_count), 0) + first == row)
                at_row[rows, :] = here
            else:
                here = at_row[rows, :]
            both = lax.dot_general(here, spread[...], NT, preferred_element_type=jnp.float32)
            both = both[:, :cells_z] + both[:, cells_z:]
            if step == 0:
                planes = pl.ds(index * (row_chunk // cells_y), row_chunk // cells_y)
                state[1, 1, planes, inside_y, :] += both.reshape(-1, cells_y, cells_z)
            else:
                inj[step, rows, :] = both
            return carry

        lax.fori_loop(0, span * cells_y // row_chunk, one_chunk, 0)

    aperture_here = aperture_ref[0, me].astype(jnp.float32)

    portions = (
        (REACH, span - 2 * REACH),
        (0, REACH),
        (span - REACH, REACH),
    )

    def image_planes(portion, row=0, rows=cells_y):
        first, count = portions[portion]
        within = pl.ds(row, rows)
        shifted = pl.ds(row + MARGIN, rows)

        def one_plane(index, carry):
            plane = index + first
            total = final[0, 0, plane, within, :] * final[1, 0, plane, within, :]
            for step in range(1, step_count):
                total = total + (
                    state[step, 0, plane, shifted, :] * state[step, 1, plane, shifted, :]
                )
            image[plane, within, :] = aperture_here * total
            return carry

        lax.fori_loop(0, count, one_plane, 0)

    def image_copies(portion, half):
        first, count = portions[portion]
        there = lax.rem(own_half + 1 - half, 2) * half_shots
        copies = []
        for turn in range(half, half_shots):
            peer = there + lax.rem(shot + turn, half_shots)
            slot = half * (half_shots - 1) + turn
            rows = pl.ds(pl.multiple_of(peer * own_rows, own_rows), own_rows)
            copies.append(
                pltpu.make_async_remote_copy(
                    src_ref=image.at[pl.ds(first, count), rows, :],
                    dst_ref=image_in.at[slot, pl.ds(first, count)],
                    send_sem=image_send.at[portion, slot],
                    recv_sem=image_recv.at[portion, slot],
                    device_id={"shot": peer},
                    device_id_type=MESH,
                )
            )
        return copies

    def image_start(portion, half):
        for copy in image_copies(portion, half):
            copy.start()

    def image_join(portion):
        first, count = portions[portion]
        for half in range(2):
            for copy in image_copies(portion, half):
                copy.wait_recv()
        rows = pl.ds(pl.multiple_of(shot * own_rows, own_rows), own_rows)

        def one_plane(index, carry):
            plane = index + first
            total = image[plane, rows, :]
            for slot in range(shot_count - 1):
                total = total + image_in[slot, plane]
            image_out[plane] = total
            return carry

        lax.fori_loop(0, count, one_plane, 0)

    last = step_count - 1

    def arrivals(step, field):
        def arrive(side):
            halo_wait(step, field, side)
            add_halo(step, field, side)
            if step < last:
                halo_start(step + 1, field, side)

        by_distance(arrive, arrive)

    for step in range(last):
        arrivals(step, 0)
        if step == 0:
            receive()
            deposit(0)
            advance(1, 0)
        else:
            advance(step + 1, 0)
            deposit(step + 1)
        arrivals(step, 1)
        if step == 0:
            deposit(1)
        if step + 1 < last:
            advance(step + 1, 1)

    along_depth(last, 1)
    for half in range(2):
        advance_rows(last, 1, halves[half], half_rows)
        if half == 0:
            image_planes(0, halves[0], half_rows)
            image_start(0, 0)

    def finish(half, side):
        half_wait(half, side)
        for field in range(2):
            add_halo(last, field, side, halves[half], half_rows)
        image_planes(1 + side, halves[half], half_rows)
        image_start(1 + side, half)

    def near(side):
        for half in range(2):
            finish(half, side)
        image_planes(0, halves[1], half_rows)
        image_start(0, 1)

    def far(side):
        finish(0, side)
        image_join(0)
        finish(1, side)
        for portion in (2 - side, 1 + side):
            image_join(portion)

    by_distance(near, far)
    for swap in swaps:
        swap.wait_send()
    for step in range(step_count):
        for field in range(2):
            for side in range(2):
                halo_sent(step, field, side)
    for portion in range(3):
        for half in range(2):
            for copy in image_copies(portion, half):
                copy.wait_send()


def write_out(image_ref, final_ref, image_hbm, final_hbm, sem):
    copies = [
        pltpu.make_async_copy(source, target, sem.at[index])
        for index, (source, target) in enumerate(
            ((final_ref, final_hbm), (image_ref, image_hbm))
        )
    ]
    for copy in copies:
        copy.start()
    for copy in copies:
        copy.wait()


def local(
    courant,
    wave_now,
    wave_later,
    traces,
    rec_owner,
    rec_cell,
    source_x,
    source_yz,
    wavelet,
    aperture,
):
    span, cells_y, cells_z = courant.shape
    sub_count = lax.axis_size("sub")
    shot_count = lax.axis_size("shot")
    step_count, receivers = traces.shape[1:]
    capacity = max(2, 2 * receivers // sub_count)
    group = max(1, min(LANES // capacity, sub_count))
    slot_count = sub_count // group * LANES
    terms_height = -(-3 * (step_count + 1) // 16) * 16
    vmem = pl.BlockSpec(memory_space=pltpu.VMEM)
    hbm = pl.BlockSpec(memory_space=pl.ANY)
    dma = pltpu.SemaphoreType.DMA
    image, final = pl.pallas_call(
        functools.partial(kernel, sub_count, shot_count, step_count),
        out_shape=(
            pltpu.VMEM((span, cells_y // shot_count, cells_z), jnp.float32),
            pltpu.VMEM(wave_now.shape, jnp.float32),
        ),
        in_specs=[hbm] * 10,
        out_specs=(vmem, vmem),
        scratch_shapes=[
            pltpu.SMEM(wavelet.shape, jnp.float32),
            pltpu.SMEM((1, 1), jnp.int32),
            pltpu.SMEM((1, 1), jnp.int32),
            pltpu.SMEM(aperture.shape, jnp.int32),
            pltpu.VMEM((1, receivers), jnp.int32),
            pltpu.VMEM((1, receivers), jnp.int32),
            pltpu.VMEM((step_count, 1, receivers), jnp.float32),
            dma((7,)),
            pltpu.VMEM(
                (step_count, 2, span, cells_y + 2 * MARGIN, cells_z), jnp.float32
            ),
            pltpu.VMEM((step_count, 2, 2, REACH, cells_y, cells_z), jnp.float32),
            pltpu.VMEM((2 * cells_z, 2 * cells_z), jnp.bfloat16),
            pltpu.VMEM((span, cells_y, cells_z), jnp.float32),
            pltpu.VMEM((2, span, cells_y, cells_z), jnp.float32),
            pltpu.VMEM((span, cells_y, cells_z), jnp.float32),
            pltpu.VMEM((step_count, span * cells_y, cells_z), jnp.float32),
            pltpu.VMEM((span, cells_y, cells_z), jnp.float32),
            pltpu.VMEM(
                (max(1, shot_count - 1), span, cells_y // shot_count, cells_z), jnp.float32
            ),
            pltpu.VMEM((terms_height, receivers), jnp.float32),
            pltpu.VMEM((terms_height, sub_count * LANES), jnp.float32),
            pltpu.VMEM((sub_count, step_count + 1, LANES), jnp.float32),
            pltpu.VMEM((sub_count, step_count + 1, LANES), jnp.float32),
            pltpu.VMEM((step_count + 1, slot_count), jnp.float32),
            pltpu.VMEM((2 * cells_z, slot_count), jnp.bfloat16),
            pltpu.VMEM((span * cells_y, slot_count), jnp.bfloat16),
            dma((4,)),
            dma((step_count, 2, 2)),
            dma((step_count, 2, 2)),
            dma((2, 2, 2)),
            dma((2, 2, 2)),
            dma((sub_count,)),
            dma((sub_count,)),
            dma((3, max(1, shot_count - 1))),
            dma((3, max(1, shot_count - 1))),
        ],
        compiler_params=pltpu.CompilerParams(
            collective_id=0, has_side_effects=True
        ),
    )(
        wavelet,
        source_x.reshape(1, 1),
        source_yz.reshape(1, 1),
        aperture,
        rec_owner.reshape(1, receivers),
        rec_cell,
        jnp.transpose(traces, (1, 0, 2)),
        courant,
        wave_now,
        wave_later,
    )
    return pl.pallas_call(
        write_out,
        out_shape=(
            jax.ShapeDtypeStruct(image.shape, jnp.float32),
            jax.ShapeDtypeStruct(final.shape, jnp.float32),
        ),
        in_specs=[vmem, vmem],
        out_specs=(hbm, hbm),
        scratch_shapes=[dma((2,))],
    )(
        pltpu.with_memory_space_constraint(image, pltpu.VMEM),
        pltpu.with_memory_space_constraint(final, pltpu.VMEM),
    )


def solution(mesh):
    in_specs = (
        P("sub", None, None),
        P(None, "shot", "sub", None, None),
        P(None, "shot", "sub", None, None),
        P("shot", None, "sub"),
        P("shot", "sub", None),
        P("shot", "sub"),
        P("shot"),
        P("shot"),
        P("shot", None),
        P("shot", None),
    )
    out_specs = (P("sub", "shot", None), P(None, "shot", "sub", None, None))
    return jax.shard_map(local, mesh=mesh, in_specs=in_specs, out_specs=out_specs, check_vma=False)
```

```python
import functools

import jax
import jax.numpy as jnp
from jax import lax
from jax.experimental import pallas as pl
from jax.experimental.pallas import tpu as pltpu
from jax.sharding import PartitionSpec as P

STENCIL = (-205.0 / 72.0, 8.0 / 5.0, -1.0 / 5.0, 8.0 / 315.0, -1.0 / 560.0)
REACH = len(STENCIL) - 1
MARGIN = 8
LANES = 128
SUBLANES = 8
MESH = pl.DeviceIdType.MESH
NT = (((1,), (1,)), ((), ()))


def iota(shape, dim):
    return lax.broadcasted_iota(jnp.int32, shape, dim)


def onehot(mask):
    return jnp.where(mask, 1.0, 0.0).astype(jnp.bfloat16)


def rounded(x):
    return x.astype(jnp.bfloat16).astype(jnp.float32)


def kernel(
    sub_count,
    shot_count,
    step_count,
    wavelet_hbm,
    source_x_hbm,
    source_yz_hbm,
    aperture_hbm,
    owner_hbm,
    cell_hbm,
    trace_hbm,
    courant_hbm,
    now_hbm,
    later_hbm,
    image_out,
    final,
    wavelet_ref,
    source_x_ref,
    source_yz_ref,
    aperture_ref,
    owner_ref,
    cell_ref,
    trace_ref,
    small_sem,
    state,
    halo,
    band,
    along,
    later,
    courant,
    inj,
    image,
    image_in,
    terms,
    packed_terms,
    packed,
    arrived,
    slots,
    spread,
    at_row,
    load_sem,
    halo_send,
    halo_recv,
    half_send,
    half_recv,
    swap_send,
    swap_recv,
    image_send,
    image_recv,
):
    span, cells_y, cells_z = courant.shape
    receivers = owner_ref.shape[1]
    capacity = max(2, 2 * receivers // sub_count)
    group = max(1, min(LANES // capacity, sub_count))
    own_rows = cells_y // shot_count
    me = lax.axis_index("sub")
    shot = lax.axis_index("shot")
    half_rows = cells_y // 2
    half_shots = shot_count // 2
    own_half = shot // half_shots
    halves = tuple(
        pl.multiple_of(half * half_rows, half_rows) for half in (1 - own_half, own_half)
    )
    has_before = me > 0
    has_after = me < sub_count - 1
    inside_y = pl.ds(MARGIN, cells_y)

    barrier = pltpu.get_barrier_semaphore()
    for offset in range(1, sub_count):
        pl.semaphore_signal(
            barrier,
            inc=1,
            device_id={"sub": lax.rem(me + offset, sub_count)},
            device_id_type=MESH,
        )
    for offset in range(1, shot_count):
        pl.semaphore_signal(
            barrier,
            inc=1,
            device_id={"shot": lax.rem(shot + offset, shot_count)},
            device_id_type=MESH,
        )

    small_loads = [
        pltpu.make_async_copy(source, target, small_sem.at[index])
        for index, (source, target) in enumerate(
            (
                (owner_hbm, owner_ref),
                (cell_hbm, cell_ref),
                (trace_hbm, trace_ref),
                (wavelet_hbm, wavelet_ref),
                (source_x_hbm, source_x_ref),
                (source_yz_hbm, source_yz_ref),
                (aperture_hbm, aperture_ref),
            )
        )
    ]
    for load in small_loads:
        load.start()
    loads = [
        pltpu.make_async_copy(
            now_hbm.at[field, 0],
            state.at[0, field, :, inside_y, :],
            load_sem.at[field],
        )
        for field in range(2)
    ]
    loads.append(pltpu.make_async_copy(later_hbm.at[:, 0], later, load_sem.at[2]))
    loads.append(pltpu.make_async_copy(courant_hbm, courant, load_sem.at[3]))
    for load in loads:
        load.start()

    def halo_copy(step, field, side):
        first = side * (span - REACH)
        if step == 0:
            source = now_hbm.at[field, 0, pl.ds(first, REACH)]
        else:
            source = state.at[step, field, pl.ds(first, REACH), inside_y, :]
        return pltpu.make_async_remote_copy(
            src_ref=source,
            dst_ref=halo.at[step, field, 1 - side],
            send_sem=halo_send.at[step, field, side],
            recv_sem=halo_recv.at[step, field, 1 - side],
            device_id={"sub": lax.rem(me + sub_count - 1 + 2 * side, sub_count)},
            device_id_type=MESH,
        )

    def half_copy(field, half, side):
        step = step_count - 1
        return pltpu.make_async_remote_copy(
            src_ref=state.at[
                step,
                field,
                pl.ds(side * (span - REACH), REACH),
                pl.ds(halves[half] + MARGIN, half_rows),
                :,
            ],
            dst_ref=halo.at[step, field, 1 - side, :, pl.ds(halves[half], half_rows), :],
            send_sem=half_send.at[field, half, side],
            recv_sem=half_recv.at[field, half, 1 - side],
            device_id={"sub": lax.rem(me + sub_count - 1 + 2 * side, sub_count)},
            device_id_type=MESH,
        )

    reaches = (has_before, has_after)

    def halo_start(step, field, side):
        @pl.when(reaches[side])
        def _():
            if step < step_count - 1:
                halo_copy(step, field, side).start()
            else:
                for other, half in ((0, 0),) if field == 0 else ((1, 0), (0, 1), (1, 1)):
                    half_copy(other, half, side).start()

    def halo_wait(step, field, side):
        @pl.when(reaches[side])
        def _():
            halo_copy(step, field, 1 - side).wait_recv()

    def half_wait(half, side):
        @pl.when(reaches[side])
        def _():
            for field in range(2):
                half_copy(field, half, 1 - side).wait_recv()

    def halo_sent(step, field, side):
        @pl.when(reaches[side])
        def _():
            if step < step_count - 1:
                halo_copy(step, field, side).wait_send()
            else:
                for half in range(2):
                    half_copy(field, half, side).wait_send()

    pl.semaphore_wait(barrier, sub_count - 1 + shot_count - 1)


    for side in range(2):
        halo_start(0, 0, side)

    def clear_margins(index, carry):
        zero = jnp.zeros((MARGIN, cells_z), jnp.float32)
        for step in range(step_count):
            for field in range(2):
                state[step, field, index, pl.ds(0, MARGIN), :] = zero
                state[step, field, index, pl.ds(MARGIN + cells_y, MARGIN), :] = zero
        return carry

    lax.fori_loop(0, span, clear_margins, 0)

    def clear_halo(side):
        for step in range(step_count):
            for field in range(2):
                for plane in range(REACH):
                    halo[step, field, side, plane] = jnp.zeros((cells_y, cells_z), jnp.float32)

    @pl.when(jnp.logical_not(has_before))
    def _():
        clear_halo(0)

    @pl.when(jnp.logical_not(has_after))
    def _():
        clear_halo(1)

    apart = jnp.abs(iota((cells_z, cells_z), 0) - iota((cells_z, cells_z), 1))
    weights = jnp.where(apart == 0, 3.0 * STENCIL[0], 0.0)
    for offset in range(1, REACH + 1):
        weights = jnp.where(apart == offset, STENCIL[offset], weights)
    for column, weight in enumerate((rounded(weights), weights - rounded(weights))):
        for first in (0, cells_z):
            band[pl.ds(first, cells_z), pl.ds(column * cells_z, cells_z)] = weight.astype(
                jnp.bfloat16
            )

    for load in small_loads:
        load.wait()
    owner = owner_ref[...]
    cell = cell_ref[...]
    named = jnp.where(iota((sub_count, receivers), 0) == owner, 1.0, 0.0)
    earlier = onehot(iota((receivers, receivers), 0) < iota((receivers, receivers), 1))
    counts = jnp.dot(named.astype(jnp.bfloat16), earlier, preferred_element_type=jnp.float32)
    ranking = jnp.sum(counts * named, axis=0, keepdims=True).astype(jnp.int32)
    slot = owner * LANES + lax.rem(me, group) * capacity + ranking
    part = trace_ref[:, 0, :]
    width = step_count + 1
    terms[...] = jnp.zeros_like(terms)
    for third in range(3):
        high = rounded(part)
        terms[pl.ds(third * width, step_count), :] = high
        part = part - high
    terms[pl.ds(step_count, 1), :] = (lax.shift_right_logical(cell, 16) * 65536).astype(jnp.float32)
    terms[pl.ds(width + step_count, 1), :] = (
        jnp.bitwise_and(lax.shift_right_logical(cell, 8), 255) * 256
    ).astype(jnp.float32)
    terms[pl.ds(2 * width + step_count, 1), :] = jnp.bitwise_and(cell, 255).astype(jnp.float32)
    stacked = terms[...].astype(jnp.bfloat16)
    chunk = 4 * LANES
    for first in range(0, sub_count * LANES, chunk):
        picks = onehot(iota((chunk, receivers), 0) + first == slot)
        packed_terms[:, pl.ds(first, chunk)] = lax.dot_general(
            stacked, picks, NT, preferred_element_type=jnp.float32
        )
    for peer in range(sub_count):
        lanes = pl.ds(peer * LANES, LANES)
        packed[peer] = (
            packed_terms[pl.ds(0, width), lanes]
            + packed_terms[pl.ds(width, width), lanes]
            + packed_terms[pl.ds(2 * width, width), lanes]
        )

    swaps = []
    for offset in range(1, sub_count):
        peer = lax.rem(me + offset, sub_count)
        swaps.append(
            pltpu.make_async_remote_copy(
                src_ref=packed.at[peer],
                dst_ref=arrived.at[offset],
                send_sem=swap_send.at[offset],
                recv_sem=swap_recv.at[offset],
                device_id={"sub": peer},
                device_id_type=MESH,
            )
        )
    for swap in swaps:
        swap.start()
    long_way = jnp.logical_or(lax.rem(me, 4) == 0, lax.rem(me, 4) == 3)
    long_way = jnp.logical_and(long_way, me > sub_count // 4)

    @pl.when(jnp.logical_not(long_way))
    def _():
        for side in range(2):
            halo_start(0, 1, side)

    arrived[0] = packed[me]

    place = iota((SUBLANES, cells_z), 0) * cells_z + iota((SUBLANES, cells_z), 1)
    source_plane = source_x_ref[0, 0] - me * span
    source_place = source_yz_ref[0, 0]

    def put(step, field, plane, rows, value):
        if step == step_count - 1:
            final[field, 0, plane, rows, :] = value
        else:
            state[step + 1, field, plane, pl.ds(rows.start + MARGIN, rows.size), :] = value

    planes_at_once = 16

    def along_depth(step, field):
        def depth_part(index, carry):
            first = pl.multiple_of(index * planes_at_once, planes_at_once)
            value = state[step, field, pl.ds(first, planes_at_once), inside_y, :]
            value = value.reshape(planes_at_once * cells_y, cells_z)
            high = value.astype(jnp.bfloat16)
            low = (value - high.astype(jnp.float32)).astype(jnp.bfloat16)
            both = jnp.dot(
                jnp.concatenate([high, low], axis=1),
                band[...],
                preferred_element_type=jnp.float32,
            )
            total = both[:, :cells_z] + both[:, cells_z:]
            along[pl.ds(first, planes_at_once)] = total.reshape(planes_at_once, cells_y, cells_z)
            return carry

        lax.fori_loop(0, span // planes_at_once, depth_part, 0)

    def advance_rows(step, field, row, count):
        def one_row(index, carry):
            first = pl.multiple_of(row + index * SUBLANES, SUBLANES)
            rows = pl.ds(first, SUBLANES)
            shifted = pl.ds(first + MARGIN, SUBLANES)
            column = [state[step, field, plane, shifted, :] for plane in range(span)]
            if field == 0:
                source_here = jnp.where(
                    place + first * cells_z == source_place, wavelet_ref[0, step], 0.0
                )
            for plane in range(span):
                total = along[plane, rows, :]
                for offset in range(1, REACH + 1):
                    near = (
                        state[step, field, plane, pl.ds(first + MARGIN + offset, SUBLANES), :]
                        + state[step, field, plane, pl.ds(first + MARGIN - offset, SUBLANES), :]
                    )
                    for other in (plane - offset, plane + offset):
                        if 0 <= other < span:
                            near = near + column[other]
                    total = total + STENCIL[offset] * near
                if step == 0:
                    past = later[field, plane, rows, :]
                else:
                    past = state[step - 1, field, plane, shifted, :]
                stepped = 2.0 * column[plane] - past + courant[plane, rows, :] * total
                if field == 0:
                    stepped = stepped - jnp.where(plane == source_plane, 1.0, 0.0) * source_here
                elif step > 0:
                    stepped = stepped + inj[step, pl.ds(plane * cells_y + first, SUBLANES), :]
                put(step, field, plane, rows, stepped)
            return carry

        lax.fori_loop(0, count // SUBLANES, one_row, 0)

    def advance(step, field):
        along_depth(step, field)
        advance_rows(step, field, 0, cells_y)

    def add_halo(step, field, side, row=0, count=cells_y):
        base = side * (span - REACH)

        def one_row(index, carry):
            first = pl.multiple_of(row + index * SUBLANES, SUBLANES)
            rows = pl.ds(first, SUBLANES)
            shifted = pl.ds(first + MARGIN, SUBLANES)
            outside = [halo[step, field, side, plane, rows, :] for plane in range(REACH)]
            for plane in range(REACH):
                total = jnp.zeros((SUBLANES, cells_z), jnp.float32)
                for other in range(REACH):
                    distance = other + REACH - plane if side else plane + REACH - other
                    if distance <= REACH:
                        total = total + STENCIL[distance] * outside[other]
                if step == step_count - 1:
                    value = final[field, 0, base + plane, rows, :]
                else:
                    value = state[step + 1, field, base + plane, shifted, :]
                value = value + courant[base + plane, rows, :] * total
                put(step, field, base + plane, rows, value)
            return carry

        lax.fori_loop(0, count // SUBLANES, one_row, 0)

    def by_distance(near, far):
        even = lax.rem(me, 2) == 0
        for act, first, second in ((near, 1, 0), (far, 0, 1)):

            @pl.when(even)
            def _(act=act, side=first):
                act(side)

            @pl.when(jnp.logical_not(even))
            def _(act=act, side=second):
                act(side)

    loads[0].wait()
    loads[2].wait()
    loads[3].wait()
    advance(0, 0)
    loads[1].wait()
    advance(0, 1)

    @pl.when(long_way)
    def _():
        for side in range(2):
            halo_start(0, 1, side)


    slot_count = slots.shape[1]

    def receive():
        for swap in swaps:
            swap.wait_recv()
        for first in range(0, sub_count, group):
            joined = arrived[first]
            for other in range(1, group):
                joined = joined + arrived[first + other]
            slots[:, pl.ds(first // group * LANES, LANES)] = joined

    def deposit(step):
        here = slots[pl.ds(step_count, 1), :].astype(jnp.int32)
        row = here // cells_z
        depth = here - row * cells_z
        at_depth = iota((cells_z, slot_count), 0) == depth
        value = slots[pl.ds(step, 1), :]
        high = rounded(value)
        low = value - high
        spread[pl.ds(0, cells_z), :] = jnp.where(at_depth, high, 0.0).astype(jnp.bfloat16)
        spread[pl.ds(cells_z, cells_z), :] = jnp.where(at_depth, low, 0.0).astype(jnp.bfloat16)
        row_chunk = 512

        def one_chunk(index, carry):
            first = pl.multiple_of(index * row_chunk, row_chunk)
            rows = pl.ds(first, row_chunk)
            if step == 0:
                here = onehot(iota((row_chunk, slot_count), 0) + first == row)
                at_row[rows, :] = here
            else:
                here = at_row[rows, :]
            both = lax.dot_general(here, spread[...], NT, preferred_element_type=jnp.float32)
            both = both[:, :cells_z] + both[:, cells_z:]
            if step == 0:
                planes = pl.ds(index * (row_chunk // cells_y), row_chunk // cells_y)
                state[1, 1, planes, inside_y, :] += both.reshape(-1, cells_y, cells_z)
            else:
                inj[step, rows, :] = both
            return carry

        lax.fori_loop(0, span * cells_y // row_chunk, one_chunk, 0)

    aperture_here = aperture_ref[0, me].astype(jnp.float32)

    portions = (
        (REACH, span - 2 * REACH),
        (0, REACH),
        (span - REACH, REACH),
    )

    def image_planes(portion, row=0, rows=cells_y):
        first, count = portions[portion]
        within = pl.ds(row, rows)
        shifted = pl.ds(row + MARGIN, rows)

        def one_plane(index, carry):
            plane = index + first
            total = final[0, 0, plane, within, :] * final[1, 0, plane, within, :]
            for step in range(1, step_count):
                total = total + (
                    state[step, 0, plane, shifted, :] * state[step, 1, plane, shifted, :]
                )
            image[plane, within, :] = aperture_here * total
            return carry

        lax.fori_loop(0, count, one_plane, 0)

    def image_copies(portion, half):
        first, count = portions[portion]
        there = lax.rem(own_half + 1 - half, 2) * half_shots
        copies = []
        for turn in range(half, half_shots):
            peer = there + lax.rem(shot + turn, half_shots)
            slot = half * (half_shots - 1) + turn
            rows = pl.ds(pl.multiple_of(peer * own_rows, own_rows), own_rows)
            copies.append(
                pltpu.make_async_remote_copy(
                    src_ref=image.at[pl.ds(first, count), rows, :],
                    dst_ref=image_in.at[slot, pl.ds(first, count)],
                    send_sem=image_send.at[portion, slot],
                    recv_sem=image_recv.at[portion, slot],
                    device_id={"shot": peer},
                    device_id_type=MESH,
                )
            )
        return copies

    def image_start(portion, half):
        for copy in image_copies(portion, half):
            copy.start()

    def image_join(portion):
        first, count = portions[portion]
        for half in range(2):
            for copy in image_copies(portion, half):
                copy.wait_recv()
        rows = pl.ds(pl.multiple_of(shot * own_rows, own_rows), own_rows)

        def one_plane(index, carry):
            plane = index + first
            total = image[plane, rows, :]
            for slot in range(shot_count - 1):
                total = total + image_in[slot, plane]
            image_out[plane] = total
            return carry

        lax.fori_loop(0, count, one_plane, 0)

    last = step_count - 1

    def arrivals(step, field):
        def arrive(side):
            halo_wait(step, field, side)
            add_halo(step, field, side)
            if step < last:
                halo_start(step + 1, field, side)

        by_distance(arrive, arrive)

    for step in range(last):
        arrivals(step, 0)
        if step == 0:
            receive()
            deposit(0)
            advance(1, 0)
        else:
            advance(step + 1, 0)
            deposit(step + 1)
        arrivals(step, 1)
        if step == 0:
            deposit(1)
        if step + 1 < last:
            advance(step + 1, 1)

    along_depth(last, 1)
    for half in range(2):
        advance_rows(last, 1, halves[half], half_rows)
        if half == 0:
            image_planes(0, halves[0], half_rows)
            image_start(0, 0)

    def finish(half, side):
        half_wait(half, side)
        for field in range(2):
            add_halo(last, field, side, halves[half], half_rows)
        image_planes(1 + side, halves[half], half_rows)
        image_start(1 + side, half)

    def near(side):
        for half in range(2):
            finish(half, side)
        image_planes(0, halves[1], half_rows)
        image_start(0, 1)

    def far(side):
        finish(0, side)
        image_join(0)
        finish(1, side)
        for portion in (2 - side, 1 + side):
            image_join(portion)

    by_distance(near, far)
    for swap in swaps:
        swap.wait_send()
    for step in range(step_count):
        for field in range(2):
            for side in range(2):
                halo_sent(step, field, side)
    for portion in range(3):
        for half in range(2):
            for copy in image_copies(portion, half):
                copy.wait_send()


def write_out(image_ref, final_ref, image_hbm, final_hbm, sem):
    copies = [
        pltpu.make_async_copy(source, target, sem.at[index])
        for index, (source, target) in enumerate(
            ((final_ref, final_hbm), (image_ref, image_hbm))
        )
    ]
    for copy in copies:
        copy.start()
    for copy in copies:
        copy.wait()


def local(
    courant,
    wave_now,
    wave_later,
    traces,
    rec_owner,
    rec_cell,
    source_x,
    source_yz,
    wavelet,
    aperture,
):
    span, cells_y, cells_z = courant.shape
    sub_count = lax.axis_size("sub")
    shot_count = lax.axis_size("shot")
    step_count, receivers = traces.shape[1:]
    capacity = max(2, 2 * receivers // sub_count)
    group = max(1, min(LANES // capacity, sub_count))
    slot_count = sub_count // group * LANES
    terms_height = -(-3 * (step_count + 1) // 16) * 16
    vmem = pl.BlockSpec(memory_space=pltpu.VMEM)
    hbm = pl.BlockSpec(memory_space=pl.ANY)
    dma = pltpu.SemaphoreType.DMA
    image, final = pl.pallas_call(
        functools.partial(kernel, sub_count, shot_count, step_count),
        out_shape=(
            pltpu.VMEM((span, cells_y // shot_count, cells_z), jnp.float32),
            pltpu.VMEM(wave_now.shape, jnp.float32),
        ),
        in_specs=[hbm] * 10,
        out_specs=(vmem, vmem),
        scratch_shapes=[
            pltpu.SMEM(wavelet.shape, jnp.float32),
            pltpu.SMEM((1, 1), jnp.int32),
            pltpu.SMEM((1, 1), jnp.int32),
            pltpu.SMEM(aperture.shape, jnp.int32),
            pltpu.VMEM((1, receivers), jnp.int32),
            pltpu.VMEM((1, receivers), jnp.int32),
            pltpu.VMEM((step_count, 1, receivers), jnp.float32),
            dma((7,)),
            pltpu.VMEM(
                (step_count, 2, span, cells_y + 2 * MARGIN, cells_z), jnp.float32
            ),
            pltpu.VMEM((step_count, 2, 2, REACH, cells_y, cells_z), jnp.float32),
            pltpu.VMEM((2 * cells_z, 2 * cells_z), jnp.bfloat16),
            pltpu.VMEM((span, cells_y, cells_z), jnp.float32),
            pltpu.VMEM((2, span, cells_y, cells_z), jnp.float32),
            pltpu.VMEM((span, cells_y, cells_z), jnp.float32),
            pltpu.VMEM((step_count, span * cells_y, cells_z), jnp.float32),
            pltpu.VMEM((span, cells_y, cells_z), jnp.float32),
            pltpu.VMEM(
                (max(1, shot_count - 1), span, cells_y // shot_count, cells_z), jnp.float32
            ),
            pltpu.VMEM((terms_height, receivers), jnp.float32),
            pltpu.VMEM((terms_height, sub_count * LANES), jnp.float32),
            pltpu.VMEM((sub_count, step_count + 1, LANES), jnp.float32),
            pltpu.VMEM((sub_count, step_count + 1, LANES), jnp.float32),
            pltpu.VMEM((step_count + 1, slot_count), jnp.float32),
            pltpu.VMEM((2 * cells_z, slot_count), jnp.bfloat16),
            pltpu.VMEM((span * cells_y, slot_count), jnp.bfloat16),
            dma((4,)),
            dma((step_count, 2, 2)),
            dma((step_count, 2, 2)),
            dma((2, 2, 2)),
            dma((2, 2, 2)),
            dma((sub_count,)),
            dma((sub_count,)),
            dma((3, max(1, shot_count - 1))),
            dma((3, max(1, shot_count - 1))),
        ],
        compiler_params=pltpu.CompilerParams(
            collective_id=0, has_side_effects=True
        ),
    )(
        wavelet,
        source_x.reshape(1, 1),
        source_yz.reshape(1, 1),
        aperture,
        rec_owner.reshape(1, receivers),
        rec_cell,
        jnp.transpose(traces, (1, 0, 2)),
        courant,
        wave_now,
        wave_later,
    )
    return pl.pallas_call(
        write_out,
        out_shape=(
            jax.ShapeDtypeStruct(image.shape, jnp.float32),
            jax.ShapeDtypeStruct(final.shape, jnp.float32),
        ),
        in_specs=[vmem, vmem],
        out_specs=(hbm, hbm),
        scratch_shapes=[dma((2,))],
    )(
        pltpu.with_memory_space_constraint(image, pltpu.VMEM),
        pltpu.with_memory_space_constraint(final, pltpu.VMEM),
    )


def solution(mesh):
    in_specs = (
        P("sub", None, None),
        P(None, "shot", "sub", None, None),
        P(None, "shot", "sub", None, None),
        P("shot", None, "sub"),
        P("shot", "sub", None),
        P("shot", "sub"),
        P("shot"),
        P("shot"),
        P("shot", None),
        P("shot", None),
    )
    out_specs = (P("sub", "shot", None), P(None, "shot", "sub", None, None))
    return jax.shard_map(local, mesh=mesh, in_specs=in_specs, out_specs=out_specs, check_vma=False)
```
